512 devices in a mesh: wide: 64 (over z, y), narrow: 8 (over x, core).
Axes of the slice: x: 4, y: 4, z: 16, core: 2. Of those that a mesh axis runs over, the one named last changes fastest.
Arguments:
- self_block: bfloat16 [2048, 256, 256], P(('wide', 'narrow')), may hold values from -6 to 6
- cross_block: bfloat16 [2048, 256, 512], P(('wide', 'narrow')), may hold values from -0.25 to 0.25
- redundant_inverse: bfloat16 [2048, 512, 512], P(('wide', 'narrow')), may hold values from -6 to 6
- link_block: bfloat16 [2048, 256, 256], P(('wide', 'narrow')), may hold values from -0.3125 to 0.3125
- projection: bfloat16 [2048, 64, 256], P(('wide', 'narrow')), may hold values from -0.375 to 0.375
- parent_far: bfloat16 [512, 256, 256], P(('wide', 'narrow')), may hold values from -6 to 6
- point_count: int32 [2048], P(('wide', 'narrow')), may hold values from 64 to 256, as said below
- box_count: int32 [512], P(('wide', 'narrow')), may hold values from 1 to 4, as said below
Outputs:
- skeleton_blocks: bfloat16 [2048, 256, 256], P(('wide', 'narrow'))
- parent_blocks: bfloat16 [512, 256, 256], P(('wide', 'narrow'))
The draws below stay inside these ranges and needn't reach their ends.
Inputs may be any that keep to these rules, and one draw needn't show every extreme that they name: `point_count`: some box has exactly 256 live points and some exactly 64; the live points of a box are its first ones. `box_count`: A device's live boxes fill its first slots; some device has all 4 slots live.
All inputs are finite; a program needn't handle non-finite values.
Results may differ from the reference program's by a relative error of at most 0.015.
Values may be sent and summed in bfloat16 or wider, within the bound.
A program may use at most 64 MiB of HBM per device.

```python
import jax
import jax.numpy as jnp
from jax import lax

K = 256
R = 512
SLOTS = 4
SWEEPS = 4
KP = 64
ROWS = 2048
N_WIDE = 64
N_NARROW = 8
DEVICES = 512


def draw_point_count(key, part):
    key_counts = jax.random.fold_in(key, 11)
    key_shuffle = jax.random.fold_in(key, 12)
    counts = jax.random.randint(key_counts, (ROWS,), K // 4, K + 1).astype(jnp.int32)
    shuffled = jax.random.permutation(key_shuffle, ROWS)
    counts = counts.at[shuffled[0]].set(K).at[shuffled[1]].set(K // 4)
    return counts.astype(jnp.int32)


def draw_box_count(key, part):
    key_counts = jax.random.fold_in(key, 21)
    key_shuffle = jax.random.fold_in(key, 22)
    counts = jax.random.randint(key_counts, (DEVICES,), 1, 3).astype(jnp.int32)
    shuffled = jax.random.permutation(key_shuffle, DEVICES)
    heavy_count = max(DEVICES // 16, 1)
    counts = counts.at[shuffled[:heavy_count]].set(SLOTS)
    return counts.astype(jnp.int32)


def level_of(own_key, dims, cuts, smallest, largest):
    def one(dim, parts):
        draws = jax.random.uniform(jax.random.fold_in(jax.random.fold_in(own_key, 6), dim), (parts,), jnp.float32, smallest / len(cuts), largest / len(cuts))
        return jnp.repeat(jnp.exp(draws), dims[dim] // parts).reshape((-1,) + (1,) * (len(dims) - dim - 1))

    level = one(*cuts[0])
    for cut in cuts[1:]:
        level = level * one(*cut)
    return level


def bell_draw(rng, dims, width, reach, split=(), kind=jnp.bfloat16):
    drawn = jax.random.normal(rng, dims, jnp.float32) * width
    if len(split) > 0:
        drawn = level_of(rng, dims, split, -0.22, 0.18) * drawn
    return jnp.clip(drawn, min=-reach, max=reach).astype(kind)


def setup_inputs(seed: int = 0) -> dict:
    key_of = jax.random.split(jax.random.key(seed), 9)
    self_block = bell_draw(key_of[0], (ROWS, K, K), 1.0, 6.0, ((0, 512),))
    cross_block = bell_draw(key_of[1], (ROWS, K, R), R ** -0.5, 0.25, ((0, 512),))
    redundant_inverse = bell_draw(key_of[2], (ROWS, R, R), 1.0, 6.0, ((0, 512),))
    link_block = bell_draw(key_of[3], (ROWS, K, K), (5 * K // 4) ** -0.5, 0.3125, ((0, 512),))
    projection = bell_draw(key_of[4], (ROWS, KP, K), K ** -0.5, 0.375, ((0, 512),))
    parent_far = bell_draw(key_of[5], (DEVICES, K, K), 1.0, 6.0, ((0, 512),))
    point_count = draw_point_count(jax.random.fold_in(key_of[8], 71), 0)
    box_count = draw_box_count(jax.random.fold_in(key_of[8], 71), 0)
    return {"self_block": self_block, "cross_block": cross_block, "redundant_inverse": redundant_inverse, "link_block": link_block, "projection": projection, "parent_far": parent_far, "point_count": point_count, "box_count": box_count}


def local_schur(items):
    block_self, block_cross, inverse_red, point_mask, live_flag = items
    carried = jnp.dot(block_cross, inverse_red, preferred_element_type=jnp.float32).astype(jnp.bfloat16)
    update = jnp.dot(carried, block_cross.T, preferred_element_type=jnp.float32)
    outer_mask = point_mask[:, None] * point_mask[None, :]
    return (live_flag * outer_mask * (block_self.astype(jnp.float32) - update)).astype(jnp.bfloat16)


def coupled_sweep(items, final_sweep):
    lower_state, lower_link, own_local, upper_state, own_link, point_mask, live_flag = items
    lowpart = jnp.dot(lower_state, lower_link, preferred_element_type=jnp.float32).astype(jnp.bfloat16)
    from_lower = jnp.dot(lower_link.T, lowpart, preferred_element_type=jnp.float32).astype(jnp.bfloat16)
    uppart = jnp.dot(upper_state, own_link.T, preferred_element_type=jnp.float32).astype(jnp.bfloat16)
    from_upper = jnp.dot(own_link, uppart, preferred_element_type=jnp.float32)
    outer_mask = point_mask[:, None] * point_mask[None, :]
    total = live_flag * outer_mask * (own_local.astype(jnp.float32) - from_lower.astype(jnp.float32) - from_upper)
    if final_sweep:
        total = total + jnp.diag(1.0 - live_flag * point_mask)
    return total.astype(jnp.bfloat16)


def compress(items):
    skeleton, interp = items
    kept_rows = jnp.dot(interp, skeleton, preferred_element_type=jnp.float32).astype(jnp.bfloat16)
    return jnp.dot(kept_rows, interp.T, preferred_element_type=jnp.float32).astype(jnp.bfloat16)


def partial_sweep(final_sweep):
    def apply_sweep(items):
        return coupled_sweep(items, final_sweep)
    return apply_sweep


def reference(self_block, cross_block, redundant_inverse, link_block, projection, parent_far, point_count, box_count):
    positions = jnp.arange(K, dtype=jnp.int32)
    point_mask = (positions[None, :] < point_count[:, None]).astype(jnp.float32)
    slot_index = jnp.arange(ROWS, dtype=jnp.int32) % SLOTS
    live_flag = (slot_index < jnp.repeat(box_count, SLOTS)).astype(jnp.float32)
    local_all = lax.map(local_schur, (self_block, cross_block, redundant_inverse, point_mask, live_flag))
    links = link_block.reshape(N_WIDE, N_NARROW, SLOTS, K, K)
    lower_link = jnp.roll(links, 1, axis=0).reshape(ROWS, K, K)
    state = local_all
    for sweep in range(SWEEPS):
        shaped = state.reshape(N_WIDE, N_NARROW, SLOTS, K, K)
        lower_state = jnp.roll(shaped, 1, axis=0).reshape(ROWS, K, K)
        upper_state = jnp.roll(shaped, -1, axis=0).reshape(ROWS, K, K)
        final_sweep = sweep == SWEEPS - 1
        state = lax.map(partial_sweep(final_sweep), (lower_state, lower_link, local_all, upper_state, link_block, point_mask, live_flag))
    skeleton_blocks = state
    children = lax.map(compress, (skeleton_blocks, projection))
    grouped = children.reshape(N_WIDE // 2, 2, N_NARROW // 2, 2, SLOTS, KP, KP)
    grouped = grouped.transpose(0, 2, 4, 1, 3, 5, 6)
    grouped = grouped.reshape(N_WIDE // 2, N_NARROW // 2, 2, 2, 2, 2, KP, KP)
    grouped = grouped.transpose(0, 2, 1, 3, 4, 5, 6, 7).reshape(DEVICES, 4, KP, KP)
    identity = jnp.eye(4, dtype=jnp.float32)
    diagonal = jnp.einsum('rcij,cd->rcidj', grouped.astype(jnp.float32), identity).reshape(DEVICES, K, K)
    parent_blocks = (parent_far.astype(jnp.float32) + diagonal).astype(jnp.bfloat16)
    return skeleton_blocks, parent_blocks
```

```python
import functools

import jax
import jax.numpy as jnp
from jax import lax
from jax.experimental import pallas as pl
from jax.experimental.pallas import tpu as pltpu
from jax.sharding import PartitionSpec as P

SWEEPS = 4
GROUP = 4
MESH = pl.DeviceIdType.MESH
F32 = jnp.float32
BF16 = jnp.bfloat16


def mm(a, b):
    return jnp.dot(a, b, preferred_element_type=F32)


def mm_t(a, b):
    return lax.dot_general(a, b, (((1,), (1,)), ((), ())), preferred_element_type=F32)


def kernel(
    n_wide,
    pc_ref,
    bc_ref,
    self_h,
    cross_h,
    inv_h,
    link_h,
    proj_h,
    far_h,
    out_ref,
    par_ref,
    cross_v,
    inv_v,
    self_v,
    loc_o,
    lnk,
    lnk_m,
    lnk_t,
    st,
    fin,
    rly,
    mo,
    r_m,
    r_s,
    cnt_o,
    cnt_i,
    prj,
    ch_o,
    ch_i,
    far_v,
    ld_sem,
    far_sem,
    own_sem,
    a2a_ss,
    a2a_rs,
    cnt_ss,
    cnt_rs,
    prj_ss,
    prj_rs,
    z_ss,
    z_rs,
    ch_ss,
    ch_rs,
):
    k = self_h.shape[1]
    half = k // 2
    w = lax.axis_index("wide")
    n = lax.axis_index("narrow")
    y = lax.rem(w, GROUP)
    base = w - y
    b = lax.rem(n, 2)
    n0 = n - b
    uy = lax.rem(y + 1, GROUP)
    oy = lax.rem(y + 2, GROUP)
    dy = lax.rem(y + 3, GROUP)
    up = (base + uy, n)
    dn = (base + dy, n)
    op = (base + oy, n)
    zu = (lax.rem(w + GROUP, n_wide), n)
    zd = (lax.rem(w + n_wide - GROUP, n_wide), n)

    def rcopy(src, dst, ssem, rsem, dev):
        return pltpu.make_async_remote_copy(
            src_ref=src,
            dst_ref=dst,
            send_sem=ssem,
            recv_sem=rsem,
            device_id=dev,
            device_id_type=MESH,
        )

    barrier = pltpu.get_barrier_semaphore()
    for i in range(GROUP):
        for c in range(2):
            if i or c:
                dev = (base + lax.rem(y + i, GROUP), n0 + lax.rem(b + c, 2))
                pl.semaphore_signal(barrier, inc=1, device_id=dev, device_id_type=MESH)
    for dev in (zu, zd):
        pl.semaphore_signal(barrier, inc=1, device_id=dev, device_id_type=MESH)

    order = (oy, uy, dy, y)
    loads = []
    for i, slot in enumerate(order):
        trio = []
        for q, (h, v) in enumerate(((cross_h, cross_v), (inv_h, inv_v), (self_h, self_v))):
            cp = pltpu.make_async_copy(h.at[slot], v.at[i], ld_sem.at[i, q])
            cp.start()
            trio.append(cp)
        loads.append(trio)

    live = bc_ref[0]
    effs = []
    for i, slot in enumerate(order):
        eff = jnp.where(slot < live, pc_ref[slot], 0)
        effs.append(eff)
        cnt_o[i] = jnp.full((8, 128), eff, jnp.int32)
    cnt_i[pl.ds(y, 1)] = jnp.full((1, 8, 128), effs[3], jnp.int32)

    def exchange(p, src_op, src_up, src_dn, dst):
        ss, rs = a2a_ss.at[p], a2a_rs.at[p]
        lo, hi = pl.ds(0, half), pl.ds(half, half)
        return (
            rcopy(src_op.at[lo], rly.at[p, 0], ss.at[0], rs.at[0], up),
            rcopy(src_op.at[hi], rly.at[p, 1], ss.at[1], rs.at[1], dn),
            rcopy(src_up, dst.at[y], ss.at[2], rs.at[2], up),
            rcopy(src_dn, dst.at[y], ss.at[3], rs.at[3], dn),
            rcopy(rly.at[p, 0], dst.at[dy, lo], ss.at[4], rs.at[4], up),
            rcopy(rly.at[p, 1], dst.at[uy, hi], ss.at[5], rs.at[5], dn),
        )

    def relay(ex, i):
        ex[i].wait_recv()
        ex[i + 4].start()

    link_x = exchange(0, link_h.at[oy], link_h.at[uy], link_h.at[dy], lnk)
    loc_x = exchange(1, loc_o.at[0], loc_o.at[1], loc_o.at[2], st.at[0])
    fin_x = exchange(2, fin.at[oy], fin.at[uy], fin.at[dy], out_ref)

    pl.semaphore_wait(barrier, 2 * GROUP + 1)

    cnt_x = []
    for i, dev in enumerate((op, up, dn)):
        cp = rcopy(cnt_o.at[i], cnt_i.at[y], cnt_ss.at[i], cnt_rs.at[i], dev)
        cnt_x.append(cp)
    for i in range(4):
        link_x[i].start()
    for cp in cnt_x:
        cp.start()
    own_link = pltpu.make_async_copy(link_h.at[y], lnk.at[y], own_sem.at[0])
    own_link.start()
    own_prj = pltpu.make_async_copy(proj_h.at[y], prj.at[y], own_sem.at[1])
    own_prj.start()
    far_cp = pltpu.make_async_copy(far_h.at[0], far_v, far_sem)
    far_cp.start()

    rows = lax.broadcasted_iota(jnp.int32, (k, k), 0)
    cols = lax.broadcasted_iota(jnp.int32, (k, k), 1)

    def schur(i):
        for cp in loads[i]:
            cp.wait()
        cross = cross_v[i]
        carried = mm(cross, inv_v[i]).astype(BF16)
        update = mm_t(carried, cross)
        inside = (rows < effs[i]) & (cols < effs[i])
        return jnp.where(inside, self_v[i].astype(F32) - update, 0.0).astype(BF16)

    for i in range(3):
        loc_o[i] = schur(i)
    relay(link_x, 0)
    relay(link_x, 1)
    for i in range(4):
        loc_x[i].start()
    st[0, pl.ds(y, 1)] = schur(3)[None]

    own_link.wait()
    for cp in cnt_x:
        cp.wait_recv()
    for i in range(2, 6):
        link_x[i].wait_recv()
    cnts = [cnt_i[j, 0:1, 0:1] for j in range(GROUP)]
    for j in range(GROUP):
        inside = rows < cnts[j]
        if j + 1 < GROUP:
            inside = inside & (cols < cnts[j + 1])
        masked = jnp.where(inside, lnk[j].astype(F32), 0.0)
        lnk_m[j] = masked.astype(BF16)
        lnk_t[j] = masked.T.astype(BF16)

    relay(loc_x, 0)
    relay(loc_x, 1)
    prj_x = []
    for i, (src, dev) in enumerate(((oy, op), (uy, up), (dy, dn))):
        cp = rcopy(proj_h.at[src], prj.at[y], prj_ss.at[i], prj_rs.at[i], dev)
        cp.start()
        prj_x.append(cp)
    for i in range(2, 6):
        loc_x[i].wait_recv()

    def lower(t, j):
        return mm(lnk_t[j], mm(st[t, j], lnk_m[j]).astype(BF16)).astype(BF16)

    def upper(state, j):
        return mm(lnk_m[j], mm(state, lnk_t[j]).astype(BF16))

    def down_copy(t):
        return rcopy(st.at[t, 0], r_s.at[t], z_ss.at[t, 0], z_rs.at[t, 0], zd)

    def up_copy(t):
        return rcopy(mo.at[t], r_m.at[t], z_ss.at[t, 1], z_rs.at[t, 1], zu)

    diag = rows == cols

    def combine(t, j, low, high):
        total = st[0, j].astype(F32) - low.astype(F32) - high
        if t == SWEEPS - 1:
            total = total + jnp.where(diag & (rows >= cnts[j]), 1.0, 0.0)
            fin[j] = total.astype(BF16)
        else:
            st[t + 1, j] = total.astype(BF16)

    own_out = pltpu.make_async_copy(fin.at[y], out_ref.at[y], own_sem.at[2])

    def give_back(j):
        @pl.when(y == j)
        def _():
            own_out.start()

        @pl.when(uy == j)
        def _():
            fin_x[2].start()

        @pl.when(dy == j)
        def _():
            fin_x[3].start()

        @pl.when(oy == j)
        def _():
            fin_x[0].start()
            fin_x[1].start()

    y_half = y // 2
    y_bit = lax.rem(y, 2)
    lane_half = lax.broadcasted_iota(jnp.int32, (1, 2 * prj.shape[1]), 1) // prj.shape[1]

    def child_copies(j):
        c = 2 * (j % 2) + b
        dev = (base + 2 * (j // 2) + y_half, n0 + y_bit)
        mine = (y == 2 * (j // 2) + y_half) & (b == y_bit)
        here = pltpu.make_async_copy(ch_o.at[j], ch_i.at[c], ch_rs.at[c])
        there = rcopy(ch_o.at[j], ch_i.at[c], ch_ss.at[j], ch_rs.at[c], dev)
        return mine, here, there

    def child(j):
        p = prj[j]
        kept = mm(p, fin[j]).astype(BF16)
        both = mm_t(kept, jnp.concatenate([p, p], axis=0))
        ch_o[j] = jnp.where(lane_half == b, both, 0.0).astype(BF16)
        mine, here, there = child_copies(j)

        @pl.when(mine)
        def _():
            here.start()

        @pl.when(jnp.logical_not(mine))
        def _():
            there.start()

    for t in range(SWEEPS):
        last = t == SWEEPS - 1
        down_copy(t).start()
        mo[t] = lower(t, 3)
        up_copy(t).start()
        lows = [lower(t, j) for j in range(3)]
        highs = [upper(st[t, j + 1], j) for j in range(3)]
        combine(t, 1, lows[0], highs[1])
        combine(t, 2, lows[1], highs[2])
        if last:
            give_back(1)
            give_back(2)
            own_prj.wait()
            for cp in prj_x:
                cp.wait_recv()
            child(1)
            child(2)

            @pl.when(y < 2)
            def _():
                relay(fin_x, 0)

            @pl.when(y >= 2)
            def _():
                relay(fin_x, 1)

        down_copy(t).wait_recv()
        combine(t, 3, lows[2], upper(r_s[t], 3))
        if last:
            give_back(3)
        up_copy(t).wait_recv()
        inside = (rows < cnts[0]) & (cols < cnts[0])
        combine(t, 0, jnp.where(inside, r_m[t].astype(F32), 0.0), highs[0])
        if last:
            give_back(0)
            child(3)
            child(0)

    @pl.when(y < 2)
    def _():
        relay(fin_x, 1)

    @pl.when(y >= 2)
    def _():
        relay(fin_x, 0)

    far_cp.wait()
    kp = prj.shape[1]
    for c in range(4):
        pltpu.make_async_copy(ch_o.at[0], ch_i.at[c], ch_rs.at[c]).wait()
        r = pl.ds(kp * c, kp)
        l = pl.ds(2 * kp * (c // 2), 2 * kp)
        far_v[r, l] = (far_v[r, l].astype(F32) + ch_i[c].astype(F32)).astype(BF16)
    par_cp = pltpu.make_async_copy(far_v, par_ref.at[0], far_sem)
    par_cp.start()

    for i in range(2, 6):
        fin_x[i].wait_recv()
    own_out.wait()
    par_cp.wait()
    for ex in (link_x, loc_x, fin_x):
        for cp in ex:
            cp.wait_send()
    for cp in cnt_x + prj_x:
        cp.wait_send()
    for t in range(SWEEPS):
        down_copy(t).wait_send()
        up_copy(t).wait_send()
    for j in range(GROUP):
        mine, _, there = child_copies(j)

        @pl.when(jnp.logical_not(mine))
        def _():
            there.wait_send()


def local(
    n_wide,
    self_block,
    cross_block,
    redundant_inverse,
    link_block,
    projection,
    parent_far,
    point_count,
    box_count,
):
    slots, k, r = cross_block.shape
    kp = projection.shape[1]
    hbm = pl.BlockSpec(memory_space=pl.ANY)
    smem = pl.BlockSpec(memory_space=pltpu.SMEM)
    dma = pltpu.SemaphoreType.DMA
    return pl.pallas_call(
        functools.partial(kernel, n_wide),
        name="skeleton",
        out_shape=(
            jax.ShapeDtypeStruct(self_block.shape, BF16),
            jax.ShapeDtypeStruct(parent_far.shape, BF16),
        ),
        in_specs=[smem, smem] + [hbm] * 6,
        out_specs=(hbm, hbm),
        scratch_shapes=[
            pltpu.VMEM((slots, k, r), BF16),
            pltpu.VMEM((slots, r, r), BF16),
            pltpu.VMEM((slots, k, k), BF16),
            pltpu.VMEM((3, k, k), BF16),
            pltpu.VMEM((GROUP, k, k), BF16),
            pltpu.VMEM((GROUP, k, k), BF16),
            pltpu.VMEM((GROUP, k, k), BF16),
            pltpu.VMEM((SWEEPS, GROUP, k, k), BF16),
            pltpu.VMEM((GROUP, k, k), BF16),
            pltpu.VMEM((3, 2, k // 2, k), BF16),
            pltpu.VMEM((SWEEPS, k, k), BF16),
            pltpu.VMEM((SWEEPS, k, k), BF16),
            pltpu.VMEM((SWEEPS, k, k), BF16),
            pltpu.VMEM((GROUP, 8, 128), jnp.int32),
            pltpu.VMEM((GROUP, 8, 128), jnp.int32),
            pltpu.VMEM((GROUP, kp, k), BF16),
            pltpu.VMEM((GROUP, kp, 2 * kp), BF16),
            pltpu.VMEM((GROUP, kp, 2 * kp), BF16),
            pltpu.VMEM((k, k), BF16),
            dma((4, 3)),
            dma,
            dma((3,)),
            dma((3, 6)),
            dma((3, 6)),
            dma((3,)),
            dma((3,)),
            dma((3,)),
            dma((3,)),
            dma((SWEEPS, 2)),
            dma((SWEEPS, 2)),
            dma((GROUP,)),
            dma((GROUP,)),
        ],
        compiler_params=pltpu.CompilerParams(
            collective_id=0, has_side_effects=True, vmem_limit_bytes=48 * 1024 * 1024
        ),
    )(
        point_count,
        box_count,
        self_block,
        cross_block,
        redundant_inverse,
        link_block,
        projection,
        parent_far,
    )


def solution(mesh):
    block = P(("wide", "narrow"), None, None)
    flat = P(("wide", "narrow"))
    return jax.shard_map(
        functools.partial(local, mesh.shape["wide"]),
        mesh=mesh,
        in_specs=(block,) * 6 + (flat,) * 2,
        out_specs=(block, block),
        check_vma=False,
    )
```

```python
import functools

import jax
import jax.numpy as jnp
from jax import lax
from jax.experimental import pallas as pl
from jax.experimental.pallas import tpu as pltpu
from jax.sharding import PartitionSpec as P

SWEEPS = 4
GROUP = 4
MESH = pl.DeviceIdType.MESH
F32 = jnp.float32
BF16 = jnp.bfloat16


def mm(a, b):
    return jnp.dot(a, b, preferred_element_type=F32)


def mm_t(a, b):
    return lax.dot_general(a, b, (((1,), (1,)), ((), ())), preferred_element_type=F32)


def kernel(
    n_wide,
    pc_h,
    bc_ref,
    self_h,
    cross_h,
    inv_h,
    link_h,
    proj_h,
    far_h,
    out_ref,
    par_ref,
    pc_ref,
    cross_v,
    inv_v,
    self_v,
    loc_o,
    lnk,
    lnk_m,
    lnk_t,
    st,
    fin,
    rly,
    mo,
    r_m,
    r_s,
    cnt_o,
    cnt_i,
    prj,
    ch_o,
    ch_i,
    far_v,
    cnt_ld,
    ld_sem,
    far_sem,
    own_sem,
    a2a_ss,
    a2a_rs,
    cnt_ss,
    cnt_rs,
    prj_ss,
    prj_rs,
    z_ss,
    z_rs,
    ch_ss,
    ch_rs,
):
    k = self_h.shape[1]
    half = k // 2
    w = lax.axis_index("wide")
    n = lax.axis_index("narrow")
    y = lax.rem(w, GROUP)
    base = w - y
    b = lax.rem(n, 2)
    n0 = n - b
    q = y // 2
    uy = lax.rem(y + 1, GROUP)
    oy = lax.rem(y + 2, GROUP)
    dy = lax.rem(y + 3, GROUP)

    def at_z(by):
        return lax.rem(base + n_wide + GROUP * by, n_wide)

    def flag(condition):
        return jnp.where(condition, 1, 0)

    up = (base + uy, n)
    dn = (base + dy, n)
    op = (base + oy, n)
    zu = (at_z(1) + y, n)
    zd = (at_z(-1) + y, n)
    to_up = (at_z(-flag(y == 0)) + uy, n)
    to_dn = (at_z(flag(y == 3)) + dy, n)
    of_up_z = at_z(-flag(y == 2))
    of_dn_z = at_z(flag(y == 1))
    of_up = (of_up_z + uy, n)
    of_dn = (of_dn_z + dy, n)

    def rcopy(src, dst, ssem, rsem, dev):
        return pltpu.make_async_remote_copy(
            src_ref=src,
            dst_ref=dst,
            send_sem=ssem,
            recv_sem=rsem,
            device_id=dev,
            device_id_type=MESH,
        )

    barrier = pltpu.get_barrier_semaphore()

    def greet(dev):
        pl.semaphore_signal(barrier, inc=1, device_id=dev, device_id_type=MESH)

    y_bit = lax.rem(y, 2)
    pair_base = at_z(2 * y_bit - 1) + y + 1 - 2 * y_bit
    for i in range(GROUP):
        for c in range(2):
            if i or c:
                greet((base + lax.rem(y + i, GROUP), n0 + lax.rem(b + c, 2)))
    greet(zu)
    greet(zd)
    greet((pair_base, n0))
    greet((pair_base, n0 + 1))

    order = (uy, dy, oy, y)
    loads = []
    for i, slot in enumerate(order):
        trio = []
        for c, (h, v) in enumerate(((cross_h, cross_v), (inv_h, inv_v), (self_h, self_v))):
            cp = pltpu.make_async_copy(h.at[slot], v.at[i], ld_sem.at[i, c])
            cp.start()
            trio.append(cp)
        loads.append(trio)
        if i == 0:
            pc_cp = pltpu.make_async_copy(pc_h, pc_ref, cnt_ld)
            pc_cp.start()

    lo, hi = pl.ds(0, half), pl.ds(half, half)

    def exchange(p, src_op, dst_op, dst_relay_up, dst_relay_dn, a, bb):
        ss, rs = a2a_ss.at[p], a2a_rs.at[p]
        return (
            rcopy(src_op.at[lo], rly.at[p, 0], ss.at[0], rs.at[0], up),
            rcopy(src_op.at[hi], rly.at[p, 1], ss.at[1], rs.at[1], dn),
            rcopy(a[0], a[1], ss.at[2], rs.at[2], a[2]),
            rcopy(bb[0], bb[1], ss.at[3], rs.at[3], bb[2]),
            rcopy(rly.at[p, 0], dst_relay_up.at[lo], ss.at[4], rs.at[4], up),
            rcopy(rly.at[p, 1], dst_relay_dn.at[hi], ss.at[5], rs.at[5], dn),
        )

    def outward(p, src_up, src_dn, src_op, dst):
        return exchange(
            p,
            src_op,
            dst.at[2],
            dst.at[2],
            dst.at[2],
            (src_up, dst.at[3], to_up),
            (src_dn, dst.at[1], to_dn),
        )

    link_x = outward(0, link_h.at[uy], link_h.at[dy], link_h.at[oy], lnk)
    loc_x = outward(1, loc_o.at[0], loc_o.at[1], loc_o.at[2], st.at[0])
    fin_x = exchange(
        2,
        fin.at[2],
        out_ref.at[y],
        out_ref.at[dy],
        out_ref.at[uy],
        (fin.at[1], out_ref.at[y], of_up),
        (fin.at[3], out_ref.at[y], of_dn),
    )

    def relay(ex, i):
        ex[i].wait_recv()
        ex[i + 4].start()

    pl.semaphore_wait(barrier, 2 * GROUP + 3)
    link_x[2].start()
    link_x[3].start()
    own_link = pltpu.make_async_copy(link_h.at[y], lnk.at[0], own_sem.at[0])
    own_link.start()
    own_prj = pltpu.make_async_copy(proj_h.at[y], prj.at[0], own_sem.at[1])
    own_prj.start()
    far_cp = pltpu.make_async_copy(far_h.at[0], far_v, far_sem)
    far_cp.start()

    pc_cp.wait()
    live = bc_ref[0]
    effs = []
    for i, slot in enumerate(order):
        eff = jnp.where(slot < live, pc_ref[slot], 0)
        effs.append(eff)
        if i < 3:
            cnt_o[i] = jnp.full((8, 128), eff, jnp.int32)
        else:
            cnt_i[0] = jnp.full((8, 128), eff, jnp.int32)

    rows = lax.broadcasted_iota(jnp.int32, (k, k), 0)
    cols = lax.broadcasted_iota(jnp.int32, (k, k), 1)

    def schur(i):
        for cp in loads[i]:
            cp.wait()
        cross = cross_v[i]
        carried = mm(cross, inv_v[i]).astype(BF16)
        update = mm_t(carried, cross)
        inside = (rows < effs[i]) & (cols < effs[i])
        return jnp.where(inside, self_v[i].astype(F32) - update, 0.0).astype(BF16)

    loc_o[0] = schur(0)
    loc_o[1] = schur(1)
    loc_x[2].start()
    loc_x[3].start()
    cnt_x = []
    for i, (rel, dev) in enumerate(((3, to_up), (1, to_dn), (2, op))):
        cp = rcopy(cnt_o.at[i], cnt_i.at[rel], cnt_ss.at[i], cnt_rs.at[i], dev)
        cp.start()
        cnt_x.append(cp)
    loc_o[2] = schur(2)
    link_x[0].start()
    link_x[1].start()
    loc_x[0].start()
    loc_x[1].start()
    st[0, 0] = schur(3)

    def origin(j):
        return lax.rem(q + j, GROUP)

    own_link.wait()
    for cp in cnt_x:
        cp.wait_recv()

    def count(j):
        return cnt_i[pl.ds(origin(j), 1), 0:1, 0:1][0]

    def prepare(j, last):
        inside = rows < count(j)
        if not last:
            inside = inside & (cols < count(j + 1))
        masked = jnp.where(inside, lnk[pl.ds(origin(j), 1)][0].astype(F32), 0.0)
        lnk_m[pl.ds(j, 1)] = masked.astype(BF16)[None]
        lnk_t[pl.ds(j, 1)] = masked.T.astype(BF16)[None]

    def state(t, j):
        if t == 0:
            return st[0, pl.ds(origin(j), 1)][0]
        return st[t, j]

    def lower(t, j):
        return mm(lnk_t[j], mm(state(t, j), lnk_m[j]).astype(BF16)).astype(BF16)

    def upper(above, j):
        return mm(lnk_m[j], mm(above, lnk_t[j]).astype(BF16))

    def down_copy(t):
        src = st.at[t, origin(0)] if t == 0 else st.at[t, 0]
        return rcopy(src, r_s.at[t], z_ss.at[t, 0], z_rs.at[t, 0], zd)

    def up_copy(t):
        return rcopy(mo.at[t], r_m.at[t], z_ss.at[t, 1], z_rs.at[t, 1], zu)

    def send_halo(t):
        down_copy(t).start()
        mo[t] = lower(t, 3)
        up_copy(t).start()

    def when_type(i, copies):
        for v in range(2):

            @pl.when(q == v)
            def _():
                copies[i + (v if i == 2 else -v)].wait_recv()

    when_type(2, link_x)
    prepare(3, True)
    prepare(0, False)
    when_type(2, loc_x)
    send_halo(0)
    when_type(3, link_x)
    prepare(1 + q, False)
    relay(link_x, 0)
    relay(link_x, 1)
    relay(loc_x, 0)
    relay(loc_x, 1)
    prj_x = []
    for i, (src, rel, dev) in enumerate(((uy, 3, to_up), (dy, 1, to_dn), (oy, 2, op))):
        cp = rcopy(proj_h.at[src], prj.at[rel], prj_ss.at[i], prj_rs.at[i], dev)
        cp.start()
        prj_x.append(cp)
    for i in (4, 5):
        link_x[i].wait_recv()
    prepare(2 - q, False)
    when_type(3, loc_x)
    for i in (4, 5):
        loc_x[i].wait_recv()

    def combine(t, j, low, high):
        own = state(0, j)
        total = own.astype(F32) - low.astype(F32) - high
        if t == SWEEPS - 1:
            total = total + jnp.where((rows == cols) & (rows >= count(j)), 1.0, 0.0)
            fin[pl.ds(origin(j), 1)] = total.astype(BF16)[None]
        else:
            st[t + 1, j] = total.astype(BF16)

    own_out = pltpu.make_async_copy(fin.at[0], out_ref.at[y], own_sem.at[2])
    kp = prj.shape[1]
    lane_half = lax.broadcasted_iota(jnp.int32, (1, 2 * kp), 1) // kp

    def child_copies(rel):
        from_y = lax.rem(y + rel, GROUP)
        from_base = (base, of_up_z, base, of_dn_z)[rel]
        c = 2 * lax.rem(from_y, 2) + b
        owner_y = 2 * (from_y // 2) + q
        dev = (from_base + owner_y, n0 + y_bit)
        mine = (from_base == base) & (owner_y == y) & (b == y_bit)
        here = pltpu.make_async_copy(ch_o.at[rel], ch_i.at[c], ch_rs.at[c])
        there = rcopy(ch_o.at[rel], ch_i.at[c], ch_ss.at[rel], ch_rs.at[c], dev)
        return mine, here, there

    def child(rel):
        p = prj[rel]
        kept = mm(p, fin[rel]).astype(BF16)
        both = mm_t(kept, jnp.concatenate([p, p], axis=0))
        ch_o[rel] = jnp.where(lane_half == b, both, 0.0).astype(BF16)
        mine, here, there = child_copies(rel)

        @pl.when(mine)
        def _():
            here.start()

        @pl.when(jnp.logical_not(mine))
        def _():
            there.start()

    for t in range(SWEEPS):
        last = t == SWEEPS - 1
        if t:
            send_halo(t)
        lows = [lower(t, j) for j in range(3)]
        highs = [upper(state(t, j + 1), j) for j in range(3)]
        combine(t, 1, lows[0], highs[1])
        combine(t, 2, lows[1], highs[2])
        if last:
            fin_x[0].start()
            fin_x[1].start()

            @pl.when(q == 0)
            def _():
                fin_x[2].start()

            @pl.when(q == 1)
            def _():
                fin_x[3].start()

            own_prj.wait()
            for cp in prj_x:
                cp.wait_recv()
            child(2)

            @pl.when(q == 0)
            def _():
                child(1)

            @pl.when(q == 1)
            def _():
                child(3)

            relay(fin_x, 0)
            relay(fin_x, 1)

        down_copy(t).wait_recv()
        combine(t, 3, lows[2], upper(r_s[t], 3))
        up_copy(t).wait_recv()
        inside = (rows < count(0)) & (cols < count(0))
        combine(t, 0, jnp.where(inside, r_m[t].astype(F32), 0.0), highs[0])

    own_out.start()

    @pl.when(q == 0)
    def _():
        fin_x[3].start()
        child(3)

    @pl.when(q == 1)
    def _():
        fin_x[2].start()
        child(1)

    child(0)
    far_cp.wait()
    for c in range(4):
        pltpu.make_async_copy(ch_o.at[0], ch_i.at[c], ch_rs.at[c]).wait()
        r = pl.ds(kp * c, kp)
        l = pl.ds(2 * kp * (c // 2), 2 * kp)
        far_v[r, l] = (far_v[r, l].astype(F32) + ch_i[c].astype(F32)).astype(BF16)
    par_cp = pltpu.make_async_copy(far_v, par_ref.at[0], far_sem)
    par_cp.start()

    for i in range(2, 6):
        fin_x[i].wait_recv()
    own_out.wait()
    par_cp.wait()
    for ex in (link_x, loc_x, fin_x):
        for cp in ex:
            cp.wait_send()
    for cp in cnt_x + prj_x:
        cp.wait_send()
    for t in range(SWEEPS):
        down_copy(t).wait_send()
        up_copy(t).wait_send()
    for rel in range(GROUP):
        mine, _, there = child_copies(rel)

        @pl.when(jnp.logical_not(mine))
        def _():
            there.wait_send()


def local(
    n_wide,
    self_block,
    cross_block,
    redundant_inverse,
    link_block,
    projection,
    parent_far,
    point_count,
    box_count,
):
    slots, k, r = cross_block.shape
    kp = projection.shape[1]
    hbm = pl.BlockSpec(memory_space=pl.ANY)
    smem = pl.BlockSpec(memory_space=pltpu.SMEM)
    dma = pltpu.SemaphoreType.DMA
    return pl.pallas_call(
        functools.partial(kernel, n_wide),
        name="skeleton",
        out_shape=(
            jax.ShapeDtypeStruct(self_block.shape, BF16),
            jax.ShapeDtypeStruct(parent_far.shape, BF16),
        ),
        in_specs=[hbm, smem] + [hbm] * 6,
        out_specs=(hbm, hbm),
        scratch_shapes=[
            pltpu.SMEM((slots,), jnp.int32),
            pltpu.VMEM((slots, k, r), BF16),
            pltpu.VMEM((slots, r, r), BF16),
            pltpu.VMEM((slots, k, k), BF16),
            pltpu.VMEM((3, k, k), BF16),
            pltpu.VMEM((GROUP, k, k), BF16),
            pltpu.VMEM((GROUP, k, k), BF16),
            pltpu.VMEM((GROUP, k, k), BF16),
            pltpu.VMEM((SWEEPS, GROUP, k, k), BF16),
            pltpu.VMEM((GROUP, k, k), BF16),
            pltpu.VMEM((3, 2, k // 2, k), BF16),
            pltpu.VMEM((SWEEPS, k, k), BF16),
            pltpu.VMEM((SWEEPS, k, k), BF16),
            pltpu.VMEM((SWEEPS, k, k), BF16),
            pltpu.VMEM((GROUP, 8, 128), jnp.int32),
            pltpu.VMEM((GROUP, 8, 128), jnp.int32),
            pltpu.VMEM((GROUP, kp, k), BF16),
            pltpu.VMEM((GROUP, kp, 2 * kp), BF16),
            pltpu.VMEM((GROUP, kp, 2 * kp), BF16),
            pltpu.VMEM((k, k), BF16),
            dma,
            dma((4, 3)),
            dma,
            dma((3,)),
            dma((3, 6)),
            dma((3, 6)),
            dma((3,)),
            dma((3,)),
            dma((3,)),
            dma((3,)),
            dma((SWEEPS, 2)),
            dma((SWEEPS, 2)),
            dma((GROUP,)),
            dma((GROUP,)),
        ],
        compiler_params=pltpu.CompilerParams(
            collective_id=0, has_side_effects=True, vmem_limit_bytes=48 * 1024 * 1024
        ),
    )(
        pltpu.with_memory_space_constraint(point_count, pltpu.HBM),
        box_count,
        *(
            pltpu.with_memory_space_constraint(x, pltpu.HBM)
            for x in (
                self_block,
                cross_block,
                redundant_inverse,
                link_block,
                projection,
                parent_far,
            )
        ),
    )


def solution(mesh):
    block = P(("wide", "narrow"), None, None)
    flat = P(("wide", "narrow"))
    return jax.shard_map(
        functools.partial(local, mesh.shape["wide"]),
        mesh=mesh,
        in_specs=(block,) * 6 + (flat,) * 2,
        out_specs=(block, block),
        check_vma=False,
    )
```

```python
import functools

import jax
import jax.numpy as jnp
from jax import lax
from jax.experimental import pallas as pl
from jax.experimental.pallas import tpu as pltpu
from jax.sharding import PartitionSpec as P

SWEEPS = 4
GROUP = 4
MESH = pl.DeviceIdType.MESH
F32 = jnp.float32
BF16 = jnp.bfloat16


def mm(a, b):
    return jnp.dot(a, b, preferred_element_type=F32)


def mm_t(a, b):
    return lax.dot_general(a, b, (((1,), (1,)), ((), ())), preferred_element_type=F32)


def kernel(
    n_wide,
    pc_h,
    bc_ref,
    self_h,
    cross_h,
    inv_h,
    link_h,
    proj_h,
    far_h,
    out_ref,
    par_ref,
    pc_ref,
    cross_v,
    inv_v,
    self_v,
    loc_o,
    lnk,
    lnk_m,
    lnk_t,
    st,
    fin,
    rly,
    mo,
    r_m,
    r_s,
    cnt_o,
    cnt_i,
    prj,
    ch_o,
    ch_i,
    far_v,
    cnt_ld,
    ld_sem,
    far_sem,
    own_sem,
    a2a_ss,
    a2a_rs,
    cnt_ss,
    cnt_rs,
    prj_ss,
    prj_rs,
    z_ss,
    z_rs,
    ch_ss,
    ch_rs,
):
    k = self_h.shape[1]
    half = k // 2
    w = lax.axis_index("wide")
    n = lax.axis_index("narrow")
    y = lax.rem(w, GROUP)
    base = w - y
    b = lax.rem(n, 2)
    n0 = n - b
    q = y // 2
    uy = lax.rem(y + 1, GROUP)
    oy = lax.rem(y + 2, GROUP)
    dy = lax.rem(y + 3, GROUP)

    def at_z(by):
        return lax.rem(base + n_wide + GROUP * by, n_wide)

    def flag(condition):
        return jnp.where(condition, 1, 0)

    up = (base + uy, n)
    dn = (base + dy, n)
    op = (base + oy, n)
    zu = (at_z(1) + y, n)
    zd = (at_z(-1) + y, n)
    to_up = (at_z(-flag(y == 0)) + uy, n)
    to_dn = (at_z(flag(y == 3)) + dy, n)
    of_up_z = at_z(-flag(y == 2))
    of_dn_z = at_z(flag(y == 1))
    of_up = (of_up_z + uy, n)
    of_dn = (of_dn_z + dy, n)

    def rcopy(src, dst, ssem, rsem, dev):
        return pltpu.make_async_remote_copy(
            src_ref=src,
            dst_ref=dst,
            send_sem=ssem,
            recv_sem=rsem,
            device_id=dev,
            device_id_type=MESH,
        )

    barrier = pltpu.get_barrier_semaphore()

    def greet(dev):
        pl.semaphore_signal(barrier, inc=1, device_id=dev, device_id_type=MESH)

    y_bit = lax.rem(y, 2)
    pair_base = at_z(2 * y_bit - 1) + y + 1 - 2 * y_bit
    for i in range(GROUP):
        for c in range(2):
            if i or c:
                greet((base + lax.rem(y + i, GROUP), n0 + lax.rem(b + c, 2)))
    greet(zu)
    greet(zd)
    greet((pair_base, n0))
    greet((pair_base, n0 + 1))

    order = (uy, dy, oy, y)
    loads = []
    for i, slot in enumerate(order):
        trio = []
        for c, (h, v) in enumerate(((cross_h, cross_v), (inv_h, inv_v), (self_h, self_v))):
            cp = pltpu.make_async_copy(h.at[slot], v.at[i], ld_sem.at[i, c])
            cp.start()
            trio.append(cp)
        loads.append(trio)
        if i == 0:
            pc_cp = pltpu.make_async_copy(pc_h, pc_ref, cnt_ld)
            pc_cp.start()

    lo, hi = pl.ds(0, half), pl.ds(half, half)

    def exchange(p, src_op, dst_op, dst_relay_up, dst_relay_dn, a, bb):
        ss, rs = a2a_ss.at[p], a2a_rs.at[p]
        return (
            rcopy(src_op.at[lo], rly.at[p, 0], ss.at[0], rs.at[0], up),
            rcopy(src_op.at[hi], rly.at[p, 1], ss.at[1], rs.at[1], dn),
            rcopy(a[0], a[1], ss.at[2], rs.at[2], a[2]),
            rcopy(bb[0], bb[1], ss.at[3], rs.at[3], bb[2]),
            rcopy(rly.at[p, 0], dst_relay_up.at[lo], ss.at[4], rs.at[4], up),
            rcopy(rly.at[p, 1], dst_relay_dn.at[hi], ss.at[5], rs.at[5], dn),
        )

    def outward(p, src_up, src_dn, src_op, dst):
        return exchange(
            p,
            src_op,
            dst.at[2],
            dst.at[2],
            dst.at[2],
            (src_up, dst.at[3], to_up),
            (src_dn, dst.at[1], to_dn),
        )

    link_x = outward(0, link_h.at[uy], link_h.at[dy], link_h.at[oy], lnk)
    loc_x = outward(1, loc_o.at[0], loc_o.at[1], loc_o.at[2], st.at[0])
    fin_x = exchange(
        2,
        fin.at[2],
        out_ref.at[y],
        out_ref.at[dy],
        out_ref.at[uy],
        (fin.at[1], out_ref.at[y], of_up),
        (fin.at[3], out_ref.at[y], of_dn),
    )

    def relay(ex, i):
        ex[i].wait_recv()
        ex[i + 4].start()

    pc_cp.wait()
    live = bc_ref[0]
    effs = []
    for i, slot in enumerate(order):
        eff = jnp.where(slot < live, pc_ref[slot], 0)
        effs.append(eff)
        if i < 3:
            cnt_o[i] = jnp.full((8, 128), eff, jnp.int32)
        else:
            cnt_i[0] = jnp.full((8, 128), eff, jnp.int32)

    pl.semaphore_wait(barrier, 2 * GROUP + 3)
    cnt_x = []
    for i, (rel, dev) in enumerate(((3, to_up), (1, to_dn), (2, op))):
        cp = rcopy(cnt_o.at[i], cnt_i.at[rel], cnt_ss.at[i], cnt_rs.at[i], dev)
        cp.start()
        cnt_x.append(cp)
    link_x[2].start()
    link_x[3].start()
    own_link = pltpu.make_async_copy(link_h.at[y], lnk.at[0], own_sem.at[0])
    own_link.start()
    own_prj = pltpu.make_async_copy(proj_h.at[y], prj.at[0], own_sem.at[1])
    own_prj.start()
    far_cp = pltpu.make_async_copy(far_h.at[0], far_v, far_sem)
    far_cp.start()

    rows = lax.broadcasted_iota(jnp.int32, (k, k), 0)
    cols = lax.broadcasted_iota(jnp.int32, (k, k), 1)

    def schur(i):
        for cp in loads[i]:
            cp.wait()
        cross = cross_v[i]
        carried = mm(cross, inv_v[i]).astype(BF16)
        update = mm_t(carried, cross)
        inside = (rows < effs[i]) & (cols < effs[i])
        return jnp.where(inside, self_v[i].astype(F32) - update, 0.0).astype(BF16)

    loc_o[0] = schur(0)
    loc_o[1] = schur(1)
    loc_x[2].start()
    loc_x[3].start()
    loc_o[2] = schur(2)
    st[0, 0] = schur(3)
    for i in (2, 3):
        link_x[i].wait_send()
    link_x[0].start()
    link_x[1].start()

    def origin(j):
        return lax.rem(q + j, GROUP)

    own_link.wait()
    for cp in cnt_x:
        cp.wait_recv()

    def count(j):
        return cnt_i[pl.ds(origin(j), 1), 0:1, 0:1][0]

    def prepare(j, last):
        inside = rows < count(j)
        if not last:
            inside = inside & (cols < count(j + 1))
        masked = jnp.where(inside, lnk[pl.ds(origin(j), 1)][0].astype(F32), 0.0)
        lnk_m[pl.ds(j, 1)] = masked.astype(BF16)[None]
        lnk_t[pl.ds(j, 1)] = masked.T.astype(BF16)[None]

    def state(t, j):
        return st[t, pl.ds(origin(j) if t == 0 else j, 1)][0]

    def at(ref, j):
        return ref[pl.ds(j, 1)][0]

    def lower(t, j):
        return mm(at(lnk_t, j), mm(state(t, j), at(lnk_m, j)).astype(BF16)).astype(BF16)

    def upper(above, j):
        return mm(at(lnk_m, j), mm(above, at(lnk_t, j)).astype(BF16))

    def down_copy(t):
        src = st.at[t, origin(0)] if t == 0 else st.at[t, 0]
        return rcopy(src, r_s.at[t], z_ss.at[t, 0], z_rs.at[t, 0], zd)

    def up_copy(t):
        return rcopy(mo.at[t], r_m.at[t], z_ss.at[t, 1], z_rs.at[t, 1], zu)

    def when_type(i, copies):
        for v in range(2):

            @pl.when(q == v)
            def _():
                copies[i + (v if i == 2 else -v)].wait_recv()

    when_type(2, link_x)
    prepare(3, True)
    prepare(0, False)
    for i in (2, 3):
        loc_x[i].wait_send()
    loc_x[0].start()
    loc_x[1].start()
    relay(link_x, 0)
    relay(link_x, 1)
    when_type(2, loc_x)
    down_copy(0).start()
    mo[0] = lower(0, 3)
    up_copy(0).start()
    when_type(3, link_x)
    prepare(1 + q, False)
    relay(loc_x, 0)
    relay(loc_x, 1)
    for i in (4, 5):
        link_x[i].wait_recv()
    prepare(2 - q, False)
    when_type(3, loc_x)
    down_copy(0).wait_recv()
    top = upper(r_s[0], 3)
    up_copy(0).wait_recv()
    for i in (4, 5):
        loc_x[i].wait_recv()

    def combine(t, j, low, high):
        total = state(0, j).astype(F32) - low.astype(F32) - high
        if t == SWEEPS - 1:
            total = total + jnp.where((rows == cols) & (rows >= count(j)), 1.0, 0.0)
            fin[pl.ds(origin(j), 1)] = total.astype(BF16)[None]
        else:
            st[t + 1, j] = total.astype(BF16)

    own_out = pltpu.make_async_copy(fin.at[0], out_ref.at[y], own_sem.at[2])
    kp = prj.shape[1]
    lane_half = lax.broadcasted_iota(jnp.int32, (1, 2 * kp), 1) // kp

    def child_copies(rel):
        from_y = lax.rem(y + rel, GROUP)
        from_base = jnp.where(rel == 1, of_up_z, jnp.where(rel == 3, of_dn_z, base))
        c = 2 * lax.rem(from_y, 2) + b
        owner_y = 2 * (from_y // 2) + q
        dev = (from_base + owner_y, n0 + y_bit)
        mine = (from_base == base) & (owner_y == y) & (b == y_bit)
        here = pltpu.make_async_copy(ch_o.at[rel], ch_i.at[c], ch_rs.at[c])
        there = rcopy(ch_o.at[rel], ch_i.at[c], ch_ss.at[rel], ch_rs.at[c], dev)
        return mine, here, there

    def child(rel):
        p = at(prj, rel)
        kept = mm(p, at(fin, rel)).astype(BF16)
        both = mm_t(kept, jnp.concatenate([p, p], axis=0))
        ch_o[pl.ds(rel, 1)] = jnp.where(lane_half == b, both, 0.0).astype(BF16)[None]
        mine, here, there = child_copies(rel)

        @pl.when(mine)
        def _():
            here.start()

        @pl.when(jnp.logical_not(mine))
        def _():
            there.start()

    def halo_low(t):
        inside = (rows < count(0)) & (cols < count(0))
        return jnp.where(inside, r_m[t].astype(F32), 0.0)

    def bottom_done(t, high):
        combine(t, 0, halo_low(t), high)
        down_copy(t + 1).start()

    def top_done(t, low, high):
        combine(t, 3, low, high)
        mo[t + 1] = lower(t + 1, 3)
        up_copy(t + 1).start()

    bottom_done(0, upper(state(0, 1), 0))
    top_done(0, lower(0, 2), top)
    prj_x = []
    for i, (src, rel, dev) in enumerate(((uy, 3, to_up), (dy, 1, to_dn), (oy, 2, op))):
        cp = rcopy(proj_h.at[src], prj.at[rel], prj_ss.at[i], prj_rs.at[i], dev)
        cp.start()
        prj_x.append(cp)
    combine(0, 1, lower(0, 0), upper(state(0, 2), 1))
    combine(0, 2, lower(0, 1), upper(state(0, 3), 2))
    for t in range(1, SWEEPS - 1):
        combine(t, 1, lower(t, 0), upper(st[t, 2], 1))
        combine(t, 2, lower(t, 1), upper(st[t, 3], 2))
        low = lower(t, 2)
        high = upper(st[t, 1], 0)
        down_copy(t).wait_recv()
        combine(t, 3, low, upper(r_s[t], 3))
        up_copy(t).wait_recv()
        combine(t, 0, halo_low(t), high)
        down_copy(t + 1).start()
        mo[t + 1] = lower(t + 1, 3)
        up_copy(t + 1).start()
    t = SWEEPS - 1
    far_pos = 2 - q
    near_pos = 1 + q
    combine(t, far_pos, lower(t, far_pos - 1), upper(state(t, far_pos + 1), far_pos))
    fin_x[0].start()
    fin_x[1].start()
    combine(t, near_pos, lower(t, near_pos - 1), upper(state(t, near_pos + 1), near_pos))
    low = lower(t, 2)
    high = upper(st[t, 1], 0)
    own_prj.wait()
    for cp in prj_x:
        cp.wait_recv()
    for i in (0, 1):
        fin_x[i].wait_send()

    def give_back(early):
        @pl.when(q == (0 if early else 1))
        def _():
            fin_x[2].start()

        @pl.when(q == (1 if early else 0))
        def _():
            fin_x[3].start()

    give_back(True)
    child(origin(1))
    child(origin(2))
    relay(fin_x, 0)
    relay(fin_x, 1)
    down_copy(t).wait_recv()
    combine(t, 3, low, upper(r_s[t], 3))
    child(origin(3))

    @pl.when(q == 0)
    def _():
        fin_x[3].start()

    up_copy(t).wait_recv()
    combine(t, 0, halo_low(t), high)
    child(origin(0))

    @pl.when(q == 1)
    def _():
        fin_x[2].start()

    own_out.start()
    far_cp.wait()
    for c in range(4):
        pltpu.make_async_copy(ch_o.at[0], ch_i.at[c], ch_rs.at[c]).wait()
        r = pl.ds(kp * c, kp)
        l = pl.ds(2 * kp * (c // 2), 2 * kp)
        far_v[r, l] = (far_v[r, l].astype(F32) + ch_i[c].astype(F32)).astype(BF16)
    par_cp = pltpu.make_async_copy(far_v, par_ref.at[0], far_sem)
    par_cp.start()

    for i in range(2, 6):
        fin_x[i].wait_recv()
    own_out.wait()
    par_cp.wait()
    for ex, left in ((link_x, (0, 1, 4, 5)), (loc_x, (0, 1, 4, 5)), (fin_x, (2, 3, 4, 5))):
        for i in left:
            ex[i].wait_send()
    for cp in cnt_x + prj_x:
        cp.wait_send()
    for t in range(SWEEPS):
        down_copy(t).wait_send()
        up_copy(t).wait_send()
    for rel in range(GROUP):
        mine, _, there = child_copies(rel)

        @pl.when(jnp.logical_not(mine))
        def _():
            there.wait_send()


def settle(out_v, par_v, out_h, par_h, sem):
    copies = (
        pltpu.make_async_copy(out_v, out_h, sem.at[0]),
        pltpu.make_async_copy(par_v, par_h, sem.at[1]),
    )
    for cp in copies:
        cp.start()
    for cp in copies:
        cp.wait()


def local(
    n_wide,
    self_block,
    cross_block,
    redundant_inverse,
    link_block,
    projection,
    parent_far,
    point_count,
    box_count,
):
    slots, k, r = cross_block.shape
    kp = projection.shape[1]
    hbm = pl.BlockSpec(memory_space=pl.ANY)
    smem = pl.BlockSpec(memory_space=pltpu.SMEM)
    dma = pltpu.SemaphoreType.DMA
    shapes = (
        jax.ShapeDtypeStruct(self_block.shape, BF16),
        jax.ShapeDtypeStruct(parent_far.shape, BF16),
    )
    results = pl.pallas_call(
        functools.partial(kernel, n_wide),
        name="skeleton",
        out_shape=shapes,
        in_specs=[hbm, smem] + [hbm] * 6,
        out_specs=(hbm, hbm),
        scratch_shapes=[
            pltpu.SMEM((slots,), jnp.int32),
            pltpu.VMEM((slots, k, r), BF16),
            pltpu.VMEM((slots, r, r), BF16),
            pltpu.VMEM((slots, k, k), BF16),
            pltpu.VMEM((3, k, k), BF16),
            pltpu.VMEM((GROUP, k, k), BF16),
            pltpu.VMEM((GROUP, k, k), BF16),
            pltpu.VMEM((GROUP, k, k), BF16),
            pltpu.VMEM((SWEEPS, GROUP, k, k), BF16),
            pltpu.VMEM((GROUP, k, k), BF16),
            pltpu.VMEM((3, 2, k // 2, k), BF16),
            pltpu.VMEM((SWEEPS, k, k), BF16),
            pltpu.VMEM((SWEEPS, k, k), BF16),
            pltpu.VMEM((SWEEPS, k, k), BF16),
            pltpu.VMEM((GROUP, 8, 128), jnp.int32),
            pltpu.VMEM((GROUP, 8, 128), jnp.int32),
            pltpu.VMEM((GROUP, kp, k), BF16),
            pltpu.VMEM((GROUP, kp, 2 * kp), BF16),
            pltpu.VMEM((GROUP, kp, 2 * kp), BF16),
            pltpu.VMEM((k, k), BF16),
            dma,
            dma((4, 3)),
            dma,
            dma((3,)),
            dma((3, 6)),
            dma((3, 6)),
            dma((3,)),
            dma((3,)),
            dma((3,)),
            dma((3,)),
            dma((SWEEPS, 2)),
            dma((SWEEPS, 2)),
            dma((GROUP,)),
            dma((GROUP,)),
        ],
        compiler_params=pltpu.CompilerParams(
            collective_id=0, has_side_effects=True, vmem_limit_bytes=48 * 1024 * 1024
        ),
    )(
        pltpu.with_memory_space_constraint(point_count, pltpu.HBM),
        box_count,
        *(
            pltpu.with_memory_space_constraint(x, pltpu.HBM)
            for x in (
                self_block,
                cross_block,
                redundant_inverse,
                link_block,
                projection,
                parent_far,
            )
        ),
    )
    return pl.pallas_call(
        settle,
        name="settle",
        out_shape=shapes,
        in_specs=[hbm] * 2,
        out_specs=(hbm, hbm),
        scratch_shapes=[dma((2,))],
    )(*(pltpu.with_memory_space_constraint(x, pltpu.VMEM) for x in results))


def solution(mesh):
    block = P(("wide", "narrow"), None, None)
    flat = P(("wide", "narrow"))
    return jax.shard_map(
        functools.partial(local, mesh.shape["wide"]),
        mesh=mesh,
        in_specs=(block,) * 6 + (flat,) * 2,
        out_specs=(block, block),
        check_vma=False,
    )
```

```python
import functools

import jax
import jax.numpy as jnp
from jax import lax
from jax.experimental import pallas as pl
from jax.experimental.pallas import tpu as pltpu
from jax.sharding import PartitionSpec as P

SWEEPS = 4
GROUP = 4
MESH = pl.DeviceIdType.MESH
F32 = jnp.float32
BF16 = jnp.bfloat16


def mm(a, b):
    return jnp.dot(a, b, preferred_element_type=F32)


def mm_t(a, b):
    return lax.dot_general(a, b, (((1,), (1,)), ((), ())), preferred_element_type=F32)


def kernel(
    n_wide,
    pc_h,
    bc_ref,
    self_h,
    cross_h,
    inv_h,
    link_h,
    proj_h,
    far_h,
    out_ref,
    par_ref,
    pc_ref,
    cross_v,
    inv_v,
    self_v,
    loc_o,
    lnk,
    lnk_m,
    lnk_t,
    st,
    fin,
    rly,
    mo,
    r_m,
    r_s,
    cnt_o,
    cnt_i,
    prj,
    ch_o,
    ch_i,
    far_v,
    edge_m,
    edge_t,
    edge_loc,
    edge_sum,
    edge_cnt,
    cnt_ld,
    ld_sem,
    far_sem,
    own_sem,
    a2a_ss,
    a2a_rs,
    cnt_ss,
    cnt_rs,
    prj_ss,
    prj_rs,
    z_ss,
    z_rs,
    ch_ss,
    ch_rs,
    last_ss,
    last_rs,
    edge_ss,
    edge_rs,
):
    k = self_h.shape[1]
    half = k // 2
    w = lax.axis_index("wide")
    n = lax.axis_index("narrow")
    y = lax.rem(w, GROUP)
    base = w - y
    b = lax.rem(n, 2)
    n0 = n - b
    q = y // 2
    uy = lax.rem(y + 1, GROUP)
    oy = lax.rem(y + 2, GROUP)
    dy = lax.rem(y + 3, GROUP)

    def at_z(by):
        return lax.rem(base + n_wide + GROUP * by, n_wide)

    def flag(condition):
        return jnp.where(condition, 1, 0)

    up = (base + uy, n)
    dn = (base + dy, n)
    op = (base + oy, n)
    zu = (at_z(1) + y, n)
    zd = (at_z(-1) + y, n)
    to_up = (at_z(-flag(y == 0)) + uy, n)
    to_dn = (at_z(flag(y == 3)) + dy, n)
    of_up_z = at_z(-flag(y == 2))
    of_dn_z = at_z(flag(y == 1))
    of_up = (of_up_z + uy, n)
    of_dn = (of_dn_z + dy, n)

    def rcopy(src, dst, ssem, rsem, dev):
        return pltpu.make_async_remote_copy(
            src_ref=src,
            dst_ref=dst,
            send_sem=ssem,
            recv_sem=rsem,
            device_id=dev,
            device_id_type=MESH,
        )

    barrier = pltpu.get_barrier_semaphore()

    def greet(dev):
        pl.semaphore_signal(barrier, inc=1, device_id=dev, device_id_type=MESH)

    y_bit = lax.rem(y, 2)
    pair_base = at_z(2 * y_bit - 1) + y + 1 - 2 * y_bit
    for i in range(GROUP):
        for c in range(2):
            if i or c:
                greet((base + lax.rem(y + i, GROUP), n0 + lax.rem(b + c, 2)))
    greet(zu)
    greet(zd)
    greet((pair_base, n0))
    greet((pair_base, n0 + 1))

    order = (uy, dy, oy, y)
    loads = []
    for i, slot in enumerate(order):
        trio = []
        for c, (h, v) in enumerate(((cross_h, cross_v), (inv_h, inv_v), (self_h, self_v))):
            cp = pltpu.make_async_copy(h.at[slot], v.at[i], ld_sem.at[i, c])
            cp.start()
            trio.append(cp)
        loads.append(trio)
        if i == 0:
            pc_cp = pltpu.make_async_copy(pc_h, pc_ref, cnt_ld)
            pc_cp.start()

    lo, hi = pl.ds(0, half), pl.ds(half, half)

    def exchange(p, src_op, dst_op, dst_relay_up, dst_relay_dn, a, bb):
        ss, rs = a2a_ss.at[p], a2a_rs.at[p]
        return (
            rcopy(src_op.at[lo], rly.at[p, 0], ss.at[0], rs.at[0], up),
            rcopy(src_op.at[hi], rly.at[p, 1], ss.at[1], rs.at[1], dn),
            rcopy(a[0], a[1], ss.at[2], rs.at[2], a[2]),
            rcopy(bb[0], bb[1], ss.at[3], rs.at[3], bb[2]),
            rcopy(rly.at[p, 0], dst_relay_up.at[lo], ss.at[4], rs.at[4], up),
            rcopy(rly.at[p, 1], dst_relay_dn.at[hi], ss.at[5], rs.at[5], dn),
        )

    def outward(p, src_up, src_dn, src_op, dst):
        return exchange(
            p,
            src_op,
            dst.at[2],
            dst.at[2],
            dst.at[2],
            (src_up, dst.at[3], to_up),
            (src_dn, dst.at[1], to_dn),
        )

    link_x = outward(0, link_h.at[uy], link_h.at[dy], link_h.at[oy], lnk)
    loc_x = outward(1, loc_o.at[0], loc_o.at[1], loc_o.at[2], st.at[0])
    fin_x = exchange(
        2,
        fin.at[2],
        out_ref.at[y],
        out_ref.at[dy],
        out_ref.at[uy],
        (fin.at[1], out_ref.at[y], of_up),
        (fin.at[3], out_ref.at[y], of_dn),
    )

    last_lo, last_hi = (
        [
            rcopy(fin.at[o, part], out_ref.at[y, part], last_ss.at[i], last_rs.at[v, i], dev)
            for v, (o, dev) in enumerate(((3, of_dn), (1, of_up)))
        ]
        for i, part in enumerate((lo, hi))
    )

    def relay(ex, i):
        ex[i].wait_recv()
        ex[i + 4].start()

    pc_cp.wait()
    live = bc_ref[0]
    effs = []
    for i, slot in enumerate(order):
        eff = jnp.where(slot < live, pc_ref[slot], 0)
        effs.append(eff)
        if i < 3:
            cnt_o[i] = jnp.full((8, 128), eff, jnp.int32)
        else:
            cnt_i[0] = jnp.full((8, 128), eff, jnp.int32)

    pl.semaphore_wait(barrier, 2 * GROUP + 3)
    cnt_x = []
    for i, (rel, dev) in enumerate(((3, to_up), (1, to_dn), (2, op))):
        cp = rcopy(cnt_o.at[i], cnt_i.at[rel], cnt_ss.at[i], cnt_rs.at[i], dev)
        cp.start()
        cnt_x.append(cp)
    link_x[2].start()
    link_x[3].start()
    own_link = pltpu.make_async_copy(link_h.at[y], lnk.at[0], own_sem.at[0])
    own_link.start()
    own_prj = pltpu.make_async_copy(proj_h.at[y], prj.at[0], own_sem.at[1])
    own_prj.start()
    far_cp = pltpu.make_async_copy(far_h.at[0], far_v, far_sem)
    far_cp.start()

    rows = lax.broadcasted_iota(jnp.int32, (k, k), 0)
    cols = lax.broadcasted_iota(jnp.int32, (k, k), 1)

    def schur(i):
        for cp in loads[i]:
            cp.wait()
        cross = cross_v[i]
        carried = mm(cross, inv_v[i]).astype(BF16)
        update = mm_t(carried, cross)
        inside = (rows < effs[i]) & (cols < effs[i])
        return jnp.where(inside, self_v[i].astype(F32) - update, 0.0).astype(BF16)

    loc_o[0] = schur(0)
    loc_o[1] = schur(1)
    loc_x[2].start()
    loc_x[3].start()
    loc_o[2] = schur(2)
    for ex in (link_x, loc_x):
        ex[0].start()
        ex[1].start()
    st[0, 0] = schur(3)

    def origin(j):
        return lax.rem(q + j, GROUP)

    own_link.wait()
    for cp in cnt_x:
        cp.wait_recv()

    def count(j):
        return cnt_i[pl.ds(origin(j), 1), 0:1, 0:1][0]

    def prepare(j, last):
        inside = rows < count(j)
        if not last:
            inside = inside & (cols < count(j + 1))
        masked = jnp.where(inside, lnk[pl.ds(origin(j), 1)][0].astype(F32), 0.0)
        lnk_m[pl.ds(j, 1)] = masked.astype(BF16)[None]
        lnk_t[pl.ds(j, 1)] = masked.T.astype(BF16)[None]

    def state(t, j):
        return st[t, pl.ds(origin(j) if t == 0 else j, 1)][0]

    def at(ref, j):
        return ref[pl.ds(j, 1)][0]

    def lower(t, j):
        return mm(at(lnk_t, j), mm(state(t, j), at(lnk_m, j)).astype(BF16)).astype(BF16)

    def upper(above, j):
        return mm(at(lnk_m, j), mm(above, at(lnk_t, j)).astype(BF16))

    def down_copy(t):
        src = st.at[0, origin(0)] if t == 0 else st.at[2, 1] if t == 3 else st.at[t, 0]
        return rcopy(src, r_s.at[t], z_ss.at[t, 0], z_rs.at[t, 0], zd)

    def up_copy(t):
        return rcopy(mo.at[t], r_m.at[t], z_ss.at[t, 1], z_rs.at[t, 1], zu)

    def when_type(i, copies):
        for v in range(2):

            @pl.when(q == v)
            def _():
                copies[i + (v if i == 2 else -v)].wait_recv()

    when_type(2, link_x)
    prepare(3, True)
    prepare(0, False)
    edge_x = [
        rcopy(src, dst, edge_ss.at[i], edge_rs.at[i], dev)
        for i, (src, dst, dev) in enumerate(
            (
                (lnk_m.at[3], edge_m.at[0], zu),
                (lnk_m.at[0], edge_m.at[1], zd),
                (cnt_i.at[origin(0)], edge_cnt, zd),
                (st.at[0, origin(3)], edge_loc, zu),
            )
        )
    ]
    for i in range(3):
        edge_x[i].start()
    when_type(2, loc_x)
    down_copy(0).start()
    mo[0] = lower(0, 3)
    up_copy(0).start()
    edge_x[3].start()
    relay(link_x, 0)
    relay(link_x, 1)
    when_type(3, link_x)
    prepare(1 + q, False)
    relay(loc_x, 0)
    relay(loc_x, 1)
    for i in (4, 5):
        link_x[i].wait_recv()
    prepare(2 - q, False)
    when_type(3, loc_x)
    down_copy(0).wait_recv()
    top = upper(r_s[0], 3)
    up_copy(0).wait_recv()
    def combine(t, j, low, high):
        total = state(0, j).astype(F32) - low.astype(F32) - high
        if t == SWEEPS - 1:
            total = total + jnp.where((rows == cols) & (rows >= count(j)), 1.0, 0.0)
            fin[pl.ds(origin(j), 1)] = total.astype(BF16)[None]
        else:
            st[t + 1, j] = total.astype(BF16)

    own_out = pltpu.make_async_copy(fin.at[0], out_ref.at[y], own_sem.at[2])
    kp = prj.shape[1]
    lane_half = lax.broadcasted_iota(jnp.int32, (1, 2 * kp), 1) // kp

    def child_copies(rel):
        from_y = lax.rem(y + rel, GROUP)
        from_base = jnp.where(rel == 1, of_up_z, jnp.where(rel == 3, of_dn_z, base))
        c = 2 * lax.rem(from_y, 2) + b
        owner_y = 2 * (from_y // 2) + q
        dev = (from_base + owner_y, n0 + y_bit)
        mine = (from_base == base) & (owner_y == y) & (b == y_bit)
        here = pltpu.make_async_copy(ch_o.at[rel], ch_i.at[c], ch_rs.at[c])
        there = rcopy(ch_o.at[rel], ch_i.at[c], ch_ss.at[rel], ch_rs.at[c], dev)
        return mine, here, there

    def child(rel):
        p = at(prj, rel)
        kept = mm(p, at(fin, rel)).astype(BF16)
        both = mm_t(kept, jnp.concatenate([p, p], axis=0))
        ch_o[pl.ds(rel, 1)] = jnp.where(lane_half == b, both, 0.0).astype(BF16)[None]
        mine, here, there = child_copies(rel)

        @pl.when(mine)
        def _():
            here.start()

        @pl.when(jnp.logical_not(mine))
        def _():
            there.start()

    def halo_low(term):
        inside = (rows < count(0)) & (cols < count(0))
        return jnp.where(inside, term.astype(F32), 0.0)

    def bottom_done(t, high):
        combine(t, 0, halo_low(r_m[t]), high)
        down_copy(t + 1).start()

    def top_done(t, low, high):
        combine(t, 3, low, high)
        mo[t + 1] = lower(t + 1, 3)
        up_copy(t + 1).start()

    @pl.when(q == 0)
    def _():
        bottom_done(0, upper(state(0, 1), 0))

    @pl.when(q == 1)
    def _():
        top_done(0, lower(0, 2), top)

    for i in (4, 5):
        loc_x[i].wait_recv()

    @pl.when(q == 0)
    def _():
        top_done(0, lower(0, 2), top)

    @pl.when(q == 1)
    def _():
        bottom_done(0, upper(state(0, 1), 0))

    prj_x = []
    for i, (src, rel, dev) in enumerate(((uy, 3, to_up), (dy, 1, to_dn), (oy, 2, op))):
        cp = rcopy(proj_h.at[src], prj.at[rel], prj_ss.at[i], prj_rs.at[i], dev)
        cp.start()
        prj_x.append(cp)
    combine(0, 1, lower(0, 0), upper(state(0, 2), 1))
    combine(0, 2, lower(0, 1), upper(state(0, 3), 2))
    combine(1, 1, lower(1, 0), upper(st[1, 2], 1))
    combine(1, 2, lower(1, 1), upper(st[1, 3], 2))
    low = lower(1, 2)
    high = upper(st[1, 1], 0)
    down_copy(1).wait_recv()
    combine(1, 3, low, upper(r_s[1], 3))
    up_copy(1).wait_recv()
    combine(1, 0, halo_low(r_m[1]), high)
    down_copy(2).start()
    down_copy(3).start()
    mo[2] = lower(2, 3)
    up_copy(2).start()
    mo[3] = lower(2, 2)
    up_copy(3).start()
    combine(2, 1, lower(2, 0), upper(st[2, 2], 1))
    combine(2, 2, lower(2, 1), upper(st[2, 3], 2))
    for cp in edge_x:
        cp.wait_recv()
    for i in range(2):
        edge_t[i] = edge_m[i].astype(F32).T.astype(BF16)
    edge_high = mm(edge_m[0], mm(st[2, 0], edge_t[0]).astype(BF16))
    edge_sum[0] = edge_loc[...].astype(F32) - edge_high
    edge_inside = (rows < edge_cnt[0:1, 0:1]) & (cols < edge_cnt[0:1, 0:1])
    edge_sum[1] = r_s[0].astype(F32) - jnp.where(edge_inside, mo[2].astype(F32), 0.0)
    high = upper(st[2, 1], 0)
    down_copy(2).wait_recv()
    combine(2, 3, mo[3], upper(r_s[2], 3))
    up_copy(2).wait_recv()
    combine(2, 0, halo_low(r_m[2]), high)
    t = SWEEPS - 1
    far_pos = 2 - q
    near_pos = 1 + q
    combine(t, far_pos, lower(t, far_pos - 1), upper(state(t, far_pos + 1), far_pos))
    fin_x[0].start()
    fin_x[1].start()
    combine(t, near_pos, lower(t, near_pos - 1), upper(state(t, near_pos + 1), near_pos))

    @pl.when(q == 0)
    def _():
        fin_x[2].start()

    @pl.when(q == 1)
    def _():
        fin_x[3].start()

    low = lower(t, 2)
    high = upper(st[t, 1], 0)
    own_prj.wait()
    for cp in prj_x:
        cp.wait_recv()
    child(origin(1))
    child(origin(2))
    down_copy(t).wait_recv()
    above = edge_sum[1] - mm(edge_m[1], mm(r_s[t], edge_t[1]).astype(BF16))
    combine(t, 3, low, upper(above.astype(BF16), 3))

    @pl.when(q == 0)
    def _():
        last_lo[0].start()
        child(3)
        last_hi[0].start()

    up_copy(t).wait_recv()
    below = (edge_sum[0] - r_m[t].astype(F32)).astype(BF16)
    below_low = mm(edge_t[0], mm(below, edge_m[0]).astype(BF16)).astype(BF16)
    combine(t, 0, halo_low(below_low), high)

    @pl.when(q == 1)
    def _():
        last_lo[1].start()
        child(1)
        last_hi[1].start()

    child(0)
    own_out.start()
    relay(fin_x, 0)
    relay(fin_x, 1)
    far_cp.wait()
    for c in range(4):
        pltpu.make_async_copy(ch_o.at[0], ch_i.at[c], ch_rs.at[c]).wait()
        r = pl.ds(kp * c, kp)
        l = pl.ds(2 * kp * (c // 2), 2 * kp)
        far_v[r, l] = (far_v[r, l].astype(F32) + ch_i[c].astype(F32)).astype(BF16)
    par_cp = pltpu.make_async_copy(far_v, par_ref.at[0], far_sem)
    par_cp.start()

    for i in (4, 5):
        fin_x[i].wait_recv()
    outer = (y == 0) | (y == GROUP - 1)

    @pl.when(outer)
    def _():
        for i in range(2):
            last_lo[i].wait_recv()
            last_hi[i].wait_recv()

    @pl.when(jnp.logical_not(outer))
    def _():
        fin_x[2].wait_recv()
        fin_x[3].wait_recv()

    own_out.wait()
    par_cp.wait()
    for ex, left in ((link_x, range(6)), (loc_x, range(6)), (fin_x, (0, 1, 4, 5))):
        for i in left:
            ex[i].wait_send()
    for v in range(2):

        @pl.when(q == v)
        def _():
            fin_x[2 + v].wait_send()
            last_lo[v].wait_send()
            last_hi[v].wait_send()

    for cp in cnt_x + prj_x:
        cp.wait_send()
    for cp in edge_x:
        cp.wait_send()
    for t in range(SWEEPS):
        down_copy(t).wait_send()
        up_copy(t).wait_send()
    for rel in range(GROUP):
        mine, _, there = child_copies(rel)

        @pl.when(jnp.logical_not(mine))
        def _():
            there.wait_send()


def settle(out_v, par_v, out_h, par_h, sem):
    copies = (
        pltpu.make_async_copy(out_v, out_h, sem.at[0]),
        pltpu.make_async_copy(par_v, par_h, sem.at[1]),
    )
    for cp in copies:
        cp.start()
    for cp in copies:
        cp.wait()


def local(
    n_wide,
    self_block,
    cross_block,
    redundant_inverse,
    link_block,
    projection,
    parent_far,
    point_count,
    box_count,
):
    slots, k, r = cross_block.shape
    kp = projection.shape[1]
    hbm = pl.BlockSpec(memory_space=pl.ANY)
    smem = pl.BlockSpec(memory_space=pltpu.SMEM)
    dma = pltpu.SemaphoreType.DMA
    shapes = (
        jax.ShapeDtypeStruct(self_block.shape, BF16),
        jax.ShapeDtypeStruct(parent_far.shape, BF16),
    )
    results = pl.pallas_call(
        functools.partial(kernel, n_wide),
        name="skeleton",
        out_shape=shapes,
        in_specs=[hbm, smem] + [hbm] * 6,
        out_specs=(hbm, hbm),
        scratch_shapes=[
            pltpu.SMEM((slots,), jnp.int32),
            pltpu.VMEM((slots, k, r), BF16),
            pltpu.VMEM((slots, r, r), BF16),
            pltpu.VMEM((slots, k, k), BF16),
            pltpu.VMEM((3, k, k), BF16),
            pltpu.VMEM((GROUP, k, k), BF16),
            pltpu.VMEM((GROUP, k, k), BF16),
            pltpu.VMEM((GROUP, k, k), BF16),
            pltpu.VMEM((SWEEPS, GROUP, k, k), BF16),
            pltpu.VMEM((GROUP, k, k), BF16),
            pltpu.VMEM((3, 2, k // 2, k), BF16),
            pltpu.VMEM((SWEEPS, k, k), BF16),
            pltpu.VMEM((SWEEPS, k, k), BF16),
            pltpu.VMEM((SWEEPS, k, k), BF16),
            pltpu.VMEM((GROUP, 8, 128), jnp.int32),
            pltpu.VMEM((GROUP, 8, 128), jnp.int32),
            pltpu.VMEM((GROUP, kp, k), BF16),
            pltpu.VMEM((GROUP, kp, 2 * kp), BF16),
            pltpu.VMEM((GROUP, kp, 2 * kp), BF16),
            pltpu.VMEM((k, k), BF16),
            pltpu.VMEM((2, k, k), BF16),
            pltpu.VMEM((2, k, k), BF16),
            pltpu.VMEM((k, k), BF16),
            pltpu.VMEM((2, k, k), F32),
            pltpu.VMEM((8, 128), jnp.int32),
            dma,
            dma((4, 3)),
            dma,
            dma((3,)),
            dma((3, 6)),
            dma((3, 6)),
            dma((3,)),
            dma((3,)),
            dma((3,)),
            dma((3,)),
            dma((SWEEPS, 2)),
            dma((SWEEPS, 2)),
            dma((GROUP,)),
            dma((GROUP,)),
            dma((2,)),
            dma((2, 2)),
            dma((4,)),
            dma((4,)),
        ],
        compiler_params=pltpu.CompilerParams(
            collective_id=0, has_side_effects=True, vmem_limit_bytes=48 * 1024 * 1024
        ),
    )(
        pltpu.with_memory_space_constraint(point_count, pltpu.HBM),
        box_count,
        *(
            pltpu.with_memory_space_constraint(x, pltpu.HBM)
            for x in (
                self_block,
                cross_block,
                redundant_inverse,
                link_block,
                projection,
                parent_far,
            )
        ),
    )
    return pl.pallas_call(
        settle,
        name="settle",
        out_shape=shapes,
        in_specs=[hbm] * 2,
        out_specs=(hbm, hbm),
        scratch_shapes=[dma((2,))],
    )(*(pltpu.with_memory_space_constraint(x, pltpu.VMEM) for x in results))


def solution(mesh):
    block = P(("wide", "narrow"), None, None)
    flat = P(("wide", "narrow"))
    return jax.shard_map(
        functools.partial(local, mesh.shape["wide"]),
        mesh=mesh,
        in_specs=(block,) * 6 + (flat,) * 2,
        out_specs=(block, block),
        check_vma=False,
    )
```

```python
import functools

import jax
import jax.numpy as jnp
from jax import lax
from jax.experimental import pallas as pl
from jax.experimental.pallas import tpu as pltpu
from jax.sharding import PartitionSpec as P

SWEEPS = 4
GROUP = 4
PIECES = 2
MESH = pl.DeviceIdType.MESH
F32 = jnp.float32
BF16 = jnp.bfloat16


def mm(a, b):
    return jnp.dot(a, b, preferred_element_type=F32)


def mm_t(a, b):
    return lax.dot_general(a, b, (((1,), (1,)), ((), ())), preferred_element_type=F32)


def kernel(
    n_wide,
    pc_h,
    bc_ref,
    self_h,
    cross_h,
    inv_h,
    link_h,
    proj_h,
    far_h,
    out_ref,
    par_ref,
    pc_ref,
    cross_v,
    inv_v,
    self_v,
    loc_o,
    lnk,
    lnk_m,
    lnk_t,
    st,
    fin,
    rly,
    mo,
    r_m,
    r_s,
    cnt_o,
    cnt_i,
    prj,
    ch_o,
    ch_i,
    far_v,
    edge_m,
    edge_t,
    edge_loc,
    edge_sum,
    edge_cnt,
    cnt_ld,
    ld_sem,
    far_sem,
    own_sem,
    a2a_ss,
    a2a_rs,
    cnt_ss,
    cnt_rs,
    prj_rs,
    z_ss,
    z_rs,
    ch_rs,
    last_rs,
    edge_ss,
    edge_rs,
):
    k = self_h.shape[1]
    half = k // 2
    w = lax.axis_index("wide")
    n = lax.axis_index("narrow")
    y = lax.rem(w, GROUP)
    base = w - y
    b = lax.rem(n, 2)
    n0 = n - b
    q = y // 2
    uy = lax.rem(y + 1, GROUP)
    oy = lax.rem(y + 2, GROUP)
    dy = lax.rem(y + 3, GROUP)

    def at_z(by):
        return lax.rem(base + n_wide + GROUP * by, n_wide)

    def flag(condition):
        return jnp.where(condition, 1, 0)

    up = (base + uy, n)
    dn = (base + dy, n)
    op = (base + oy, n)
    zu = (at_z(1) + y, n)
    zd = (at_z(-1) + y, n)
    to_up = (at_z(-flag(y == 0)) + uy, n)
    to_dn = (at_z(flag(y == 3)) + dy, n)
    of_up_z = at_z(-flag(y == 2))
    of_dn_z = at_z(flag(y == 1))
    of_up = (of_up_z + uy, n)
    of_dn = (of_dn_z + dy, n)

    def rcopy(src, dst, ssem, rsem, dev):
        return pltpu.make_async_remote_copy(
            src_ref=src,
            dst_ref=dst,
            send_sem=ssem,
            recv_sem=rsem,
            device_id=dev,
            device_id_type=MESH,
        )

    barrier = pltpu.get_barrier_semaphore()

    def greet(dev):
        pl.semaphore_signal(barrier, inc=1, device_id=dev, device_id_type=MESH)

    y_bit = lax.rem(y, 2)
    pair_base = at_z(2 * y_bit - 1) + y + 1 - 2 * y_bit
    for i in range(GROUP):
        for c in range(2):
            if i or c:
                greet((base + lax.rem(y + i, GROUP), n0 + lax.rem(b + c, 2)))
    greet(zu)
    greet(zd)
    greet((pair_base, n0))
    greet((pair_base, n0 + 1))

    order = (uy, dy, oy, y)
    loads = []
    for i, slot in enumerate(order):
        trio = []
        for c, (h, v) in enumerate(((cross_h, cross_v), (inv_h, inv_v), (self_h, self_v))):
            cp = pltpu.make_async_copy(h.at[slot], v.at[i], ld_sem.at[i, c])
            cp.start()
            trio.append(cp)
        loads.append(trio)
        if i == 0:
            pc_cp = pltpu.make_async_copy(pc_h, pc_ref, cnt_ld)
            pc_cp.start()

    lo, hi = pl.ds(0, half), pl.ds(half, half)

    def exchange(p, src_op, dst_op, dst_relay_up, dst_relay_dn, a, bb):
        ss, rs = a2a_ss.at[p % 2], a2a_rs.at[p]
        first, second = [], []
        for i in range(2 * PIECES):
            way, piece = i % 2, i // 2
            rows_of = pl.ds(way * half + piece * (half // PIECES), half // PIECES)
            held = rly.at[p, way, pl.ds(piece * (half // PIECES), half // PIECES)]
            dev, dst = ((up, dst_relay_up), (dn, dst_relay_dn))[way]
            first.append(rcopy(src_op.at[rows_of], held, ss.at[2 + i], rs.at[2 + i], dev))
            o = 2 + 2 * PIECES + i
            second.append(rcopy(held, dst.at[rows_of], ss.at[2 + i], rs.at[o], dev))
        return {
            2: rcopy(a[0], a[1], ss.at[0], rs.at[0], a[2]),
            3: rcopy(bb[0], bb[1], ss.at[1], rs.at[1], bb[2]),
            "first": first,
            "second": second,
        }

    def outward(p, src_up, src_dn, src_op, dst):
        return exchange(
            p,
            src_op,
            dst.at[2],
            dst.at[2],
            dst.at[2],
            (src_up, dst.at[3], to_up),
            (src_dn, dst.at[1], to_dn),
        )

    link_x = outward(0, link_h.at[uy], link_h.at[dy], link_h.at[oy], lnk)
    loc_x = outward(1, loc_o.at[0], loc_o.at[1], loc_o.at[2], st.at[0])
    fin_x = exchange(
        2,
        fin.at[2],
        out_ref.at[y],
        out_ref.at[dy],
        out_ref.at[uy],
        (fin.at[1], out_ref.at[y], of_up),
        (fin.at[3], out_ref.at[y], of_dn),
    )

    last_lo, last_hi = (
        [
            rcopy(fin.at[o, part], out_ref.at[y, part], a2a_ss.at[1, i], last_rs.at[v, i], dev)
            for v, (o, dev) in enumerate(((3, of_dn), (1, of_up)))
        ]
        for i, part in enumerate((lo, hi))
    )

    def relay(ex):
        for a, b_ in zip(ex["first"], ex["second"]):
            a.wait_recv()
            a.wait_send()
            b_.start()

    pc_cp.wait()
    live = bc_ref[0]
    effs = []
    for i, slot in enumerate(order):
        eff = jnp.where(slot < live, pc_ref[slot], 0)
        effs.append(eff)
        if i < 3:
            cnt_o[i] = jnp.full((8, 128), eff, jnp.int32)
        else:
            cnt_i[0] = jnp.full((8, 128), eff, jnp.int32)

    pl.semaphore_wait(barrier, 2 * GROUP + 3)
    cnt_x = []
    for i, (rel, dev) in enumerate(((3, to_up), (1, to_dn), (2, op))):
        cp = rcopy(cnt_o.at[i], cnt_i.at[rel], cnt_ss.at[i], cnt_rs.at[i], dev)
        cp.start()
        cnt_x.append(cp)
    link_x[2].start()
    link_x[3].start()
    own_link = pltpu.make_async_copy(link_h.at[y], lnk.at[0], own_sem.at[0])
    own_link.start()
    own_prj = pltpu.make_async_copy(proj_h.at[y], prj.at[0], own_sem.at[1])
    own_prj.start()
    far_cp = pltpu.make_async_copy(far_h.at[0], far_v, far_sem)
    far_cp.start()

    rows = lax.broadcasted_iota(jnp.int32, (k, k), 0)
    cols = lax.broadcasted_iota(jnp.int32, (k, k), 1)

    def schur(i):
        for cp in loads[i]:
            cp.wait()
        cross = cross_v[i]
        carried = mm(cross, inv_v[i]).astype(BF16)
        update = mm_t(carried, cross)
        inside = (rows < effs[i]) & (cols < effs[i])
        return jnp.where(inside, self_v[i].astype(F32) - update, 0.0).astype(BF16)

    loc_o[0] = schur(0)
    loc_o[1] = schur(1)
    loc_x[2].start()
    loc_x[3].start()
    loc_o[2] = schur(2)
    for ex in (link_x, loc_x):
        for cp in ex["first"]:
            cp.start()
    st[0, 0] = schur(3)

    def origin(j):
        return lax.rem(q + j, GROUP)

    own_link.wait()
    for cp in cnt_x:
        cp.wait_recv()

    def count(j):
        return cnt_i[pl.ds(origin(j), 1), 0:1, 0:1][0]

    def prepare(j, last):
        inside = rows < count(j)
        if not last:
            inside = inside & (cols < count(j + 1))
        masked = jnp.where(inside, lnk[pl.ds(origin(j), 1)][0].astype(F32), 0.0)
        lnk_m[pl.ds(j, 1)] = masked.astype(BF16)[None]
        lnk_t[pl.ds(j, 1)] = masked.T.astype(BF16)[None]

    def state(t, j):
        return st[t, pl.ds(origin(j) if t == 0 else j, 1)][0]

    def at(ref, j):
        return ref[pl.ds(j, 1)][0]

    def lower(t, j):
        return mm(at(lnk_t, j), mm(state(t, j), at(lnk_m, j)).astype(BF16)).astype(BF16)

    def upper(above, j):
        return mm(at(lnk_m, j), mm(above, at(lnk_t, j)).astype(BF16))

    def down_copy(t):
        src = st.at[0, origin(0)] if t == 0 else st.at[2, 1] if t == 3 else st.at[t, 0]
        return rcopy(src, r_s.at[t], z_ss.at[t % 2, 0], z_rs.at[t, 0], zd)

    def up_copy(t):
        return rcopy(mo.at[t], r_m.at[t], z_ss.at[t % 2, 1], z_rs.at[t, 1], zu)

    def when_type(i, copies):
        for v in range(2):

            @pl.when(q == v)
            def _():
                copies[i + (v if i == 2 else -v)].wait_recv()

    when_type(2, link_x)
    prepare(3, True)
    prepare(0, False)
    edge_x = [
        rcopy(src, dst, edge_ss.at[i], edge_rs.at[i], dev)
        for i, (src, dst, dev) in enumerate(
            (
                (lnk_m.at[3], edge_m.at[0], zu),
                (lnk_m.at[0], edge_m.at[1], zd),
                (cnt_i.at[origin(0)], edge_cnt, zd),
                (st.at[0, origin(3)], edge_loc, zu),
            )
        )
    ]
    edge_x[0].start()
    when_type(2, loc_x)
    down_copy(0).start()
    mo[0] = lower(0, 3)
    up_copy(0).start()
    edge_x[3].start()
    edge_x[1].start()
    edge_x[2].start()
    relay(link_x)
    when_type(3, link_x)
    prepare(1 + q, False)
    relay(loc_x)
    for cp in link_x["second"]:
        cp.wait_recv()
    prepare(2 - q, False)
    when_type(3, loc_x)
    down_copy(0).wait_recv()
    top = upper(r_s[0], 3)
    up_copy(0).wait_recv()
    def combine(t, j, low, high):
        total = state(0, j).astype(F32) - low.astype(F32) - high
        if t == SWEEPS - 1:
            total = total + jnp.where((rows == cols) & (rows >= count(j)), 1.0, 0.0)
            fin[pl.ds(origin(j), 1)] = total.astype(BF16)[None]
        else:
            st[t + 1, j] = total.astype(BF16)

    own_out = pltpu.make_async_copy(fin.at[0], out_ref.at[y], own_sem.at[2])
    kp = prj.shape[1]
    lane_half = lax.broadcasted_iota(jnp.int32, (1, 2 * kp), 1) // kp

    def child_copies(rel):
        from_y = lax.rem(y + rel, GROUP)
        from_base = jnp.where(rel == 1, of_up_z, jnp.where(rel == 3, of_dn_z, base))
        c = 2 * lax.rem(from_y, 2) + b
        owner_y = 2 * (from_y // 2) + q
        dev = (from_base + owner_y, n0 + y_bit)
        mine = (from_base == base) & (owner_y == y) & (b == y_bit)
        here = pltpu.make_async_copy(ch_o.at[rel], ch_i.at[c], ch_rs.at[c])
        there = rcopy(ch_o.at[rel], ch_i.at[c], a2a_ss.at[1, 2 + rel], ch_rs.at[c], dev)
        return mine, here, there

    def children(*rels):
        for rel in rels:
            p = at(prj, rel)
            kept = mm(p, at(fin, rel)).astype(BF16)
            both = mm_t(kept, jnp.concatenate([p, p], axis=0))
            ch_o[pl.ds(rel, 1)] = jnp.where(lane_half == b, both, 0.0).astype(BF16)[None]
        for rel in rels:
            send_child(*child_copies(rel))

    def send_child(mine, here, there):
        @pl.when(mine)
        def _():
            here.start()

        @pl.when(jnp.logical_not(mine))
        def _():
            there.start()

    def halo_low(term):
        inside = (rows < count(0)) & (cols < count(0))
        return jnp.where(inside, term.astype(F32), 0.0)

    def bottom_done(t, high):
        combine(t, 0, halo_low(r_m[t]), high)
        down_copy(t + 1).start()

    def top_done(t, low, high):
        combine(t, 3, low, high)
        mo[t + 1] = lower(t + 1, 3)
        up_copy(t + 1).start()

    @pl.when(q == 0)
    def _():
        bottom_done(0, upper(state(0, 1), 0))

    @pl.when(q == 1)
    def _():
        top_done(0, lower(0, 2), top)

    for cp in loc_x["second"]:
        cp.wait_recv()

    @pl.when(q == 0)
    def _():
        top_done(0, lower(0, 2), top)

    @pl.when(q == 1)
    def _():
        bottom_done(0, upper(state(0, 1), 0))

    for cp in cnt_x:
        cp.wait_send()
    prj_x = []
    for i, (src, rel, dev) in enumerate(((uy, 3, to_up), (dy, 1, to_dn), (oy, 2, op))):
        cp = rcopy(proj_h.at[src], prj.at[rel], cnt_ss.at[i], prj_rs.at[i], dev)
        cp.start()
        prj_x.append(cp)
    combine(0, 1, lower(0, 0), upper(state(0, 2), 1))
    combine(0, 2, lower(0, 1), upper(state(0, 3), 2))
    combine(1, 1, lower(1, 0), upper(st[1, 2], 1))
    combine(1, 2, lower(1, 1), upper(st[1, 3], 2))
    low = lower(1, 2)
    high = upper(st[1, 1], 0)
    mo[3] = lower(2, 2)
    for ex in (link_x, loc_x):
        for cp in [ex[2], ex[3]] + ex["second"]:
            cp.wait_send()
    down_copy(1).wait_recv()
    combine(1, 3, low, upper(r_s[1], 3))
    mo[2] = lower(2, 3)
    for v in range(2):
        up_copy(v).wait_send()
    up_copy(2).start()
    up_copy(3).start()
    up_copy(1).wait_recv()
    combine(1, 0, halo_low(r_m[1]), high)
    for v in range(2):
        down_copy(v).wait_send()
    down_copy(2).start()
    down_copy(3).start()
    combine(2, 1, lower(2, 0), upper(st[2, 2], 1))
    combine(2, 2, lower(2, 1), upper(st[2, 3], 2))
    for cp in edge_x:
        cp.wait_recv()
    for i in range(2):
        edge_t[i] = edge_m[i].astype(F32).T.astype(BF16)
    edge_high = mm(edge_m[0], mm(st[2, 0], edge_t[0]).astype(BF16))
    edge_sum[0] = edge_loc[...].astype(F32) - edge_high
    edge_inside = (rows < edge_cnt[0:1, 0:1]) & (cols < edge_cnt[0:1, 0:1])
    edge_sum[1] = r_s[0].astype(F32) - jnp.where(edge_inside, mo[2].astype(F32), 0.0)
    high = upper(st[2, 1], 0)
    t = SWEEPS - 1

    def interior(j):
        combine(t, j, lower(t, j - 1), upper(st[t, j + 1], j))

    def new_top():
        down_copy(2).wait_recv()
        combine(2, 3, mo[3], upper(r_s[2], 3))

    def new_bottom():
        up_copy(2).wait_recv()
        combine(2, 0, halo_low(r_m[2]), high)

    def far_back():
        for cp in fin_x["first"]:
            cp.start()

    @pl.when(q == 0)
    def _():
        new_top()
        interior(2)
        far_back()
        new_bottom()
        interior(1)
        fin_x[2].start()

    @pl.when(q == 1)
    def _():
        new_bottom()
        interior(1)
        far_back()
        new_top()
        interior(2)
        fin_x[3].start()

    low = lower(t, 2)
    high = upper(st[t, 1], 0)
    own_prj.wait()
    for cp in prj_x:
        cp.wait_recv()
    children(origin(1), origin(2))
    down_copy(t).wait_recv()
    above = edge_sum[1] - mm(edge_m[1], mm(r_s[t], edge_t[1]).astype(BF16))
    combine(t, 3, low, upper(above.astype(BF16), 3))

    @pl.when(q == 0)
    def _():
        last_lo[0].start()
        children(3)
        last_hi[0].start()

    up_copy(t).wait_recv()
    below = (edge_sum[0] - r_m[t].astype(F32)).astype(BF16)
    below_low = mm(edge_t[0], mm(below, edge_m[0]).astype(BF16)).astype(BF16)
    combine(t, 0, halo_low(below_low), high)

    @pl.when(q == 1)
    def _():
        last_lo[1].start()
        children(1)
        last_hi[1].start()

    children(0)
    own_out.start()
    relay(fin_x)
    far_cp.wait()
    for c in range(4):
        pltpu.make_async_copy(ch_o.at[0], ch_i.at[c], ch_rs.at[c]).wait()
        r = pl.ds(kp * c, kp)
        l = pl.ds(2 * kp * (c // 2), 2 * kp)
        far_v[r, l] = (far_v[r, l].astype(F32) + ch_i[c].astype(F32)).astype(BF16)
    par_cp = pltpu.make_async_copy(far_v, par_ref.at[0], far_sem)
    par_cp.start()

    for cp in fin_x["second"]:
        cp.wait_recv()
    outer = (y == 0) | (y == GROUP - 1)

    @pl.when(outer)
    def _():
        for i in range(2):
            last_lo[i].wait_recv()
            last_hi[i].wait_recv()

    @pl.when(jnp.logical_not(outer))
    def _():
        fin_x[2].wait_recv()
        fin_x[3].wait_recv()

    own_out.wait()
    par_cp.wait()
    for cp in fin_x["second"]:
        cp.wait_send()
    for v in range(2):

        @pl.when(q == v)
        def _():
            fin_x[2 + v].wait_send()
            last_lo[v].wait_send()
            last_hi[v].wait_send()

    for cp in prj_x:
        cp.wait_send()
    for cp in edge_x:
        cp.wait_send()
    for t in range(2, SWEEPS):
        down_copy(t).wait_send()
        up_copy(t).wait_send()
    for rel in range(GROUP):
        mine, _, there = child_copies(rel)

        @pl.when(jnp.logical_not(mine))
        def _():
            there.wait_send()


def settle(out_v, par_v, out_h, par_h, sem):
    copies = (
        pltpu.make_async_copy(out_v, out_h, sem.at[0]),
        pltpu.make_async_copy(par_v, par_h, sem.at[1]),
    )
    for cp in copies:
        cp.start()
    for cp in copies:
        cp.wait()


def local(
    n_wide,
    self_block,
    cross_block,
    redundant_inverse,
    link_block,
    projection,
    parent_far,
    point_count,
    box_count,
):
    slots, k, r = cross_block.shape
    kp = projection.shape[1]
    hbm = pl.BlockSpec(memory_space=pl.ANY)
    smem = pl.BlockSpec(memory_space=pltpu.SMEM)
    dma = pltpu.SemaphoreType.DMA
    shapes = (
        jax.ShapeDtypeStruct(self_block.shape, BF16),
        jax.ShapeDtypeStruct(parent_far.shape, BF16),
    )
    results = pl.pallas_call(
        functools.partial(kernel, n_wide),
        name="skeleton",
        out_shape=shapes,
        in_specs=[hbm, smem] + [hbm] * 6,
        out_specs=(hbm, hbm),
        scratch_shapes=[
            pltpu.SMEM((slots,), jnp.int32),
            pltpu.VMEM((slots, k, r), BF16),
            pltpu.VMEM((slots, r, r), BF16),
            pltpu.VMEM((slots, k, k), BF16),
            pltpu.VMEM((3, k, k), BF16),
            pltpu.VMEM((GROUP, k, k), BF16),
            pltpu.VMEM((GROUP, k, k), BF16),
            pltpu.VMEM((GROUP, k, k), BF16),
            pltpu.VMEM((SWEEPS, GROUP, k, k), BF16),
            pltpu.VMEM((GROUP, k, k), BF16),
            pltpu.VMEM((3, 2, k // 2, k), BF16),
            pltpu.VMEM((SWEEPS, k, k), BF16),
            pltpu.VMEM((SWEEPS, k, k), BF16),
            pltpu.VMEM((SWEEPS, k, k), BF16),
            pltpu.VMEM((GROUP, 8, 128), jnp.int32),
            pltpu.VMEM((GROUP, 8, 128), jnp.int32),
            pltpu.VMEM((GROUP, kp, k), BF16),
            pltpu.VMEM((GROUP, kp, 2 * kp), BF16),
            pltpu.VMEM((GROUP, kp, 2 * kp), BF16),
            pltpu.VMEM((k, k), BF16),
            pltpu.VMEM((2, k, k), BF16),
            pltpu.VMEM((2, k, k), BF16),
            pltpu.VMEM((k, k), BF16),
            pltpu.VMEM((2, k, k), F32),
            pltpu.VMEM((8, 128), jnp.int32),
            dma,
            dma((4, 3)),
            dma,
            dma((3,)),
            dma((2, 2 + 2 * PIECES)),
            dma((3, 2 + 4 * PIECES)),
            dma((3,)),
            dma((3,)),
            dma((3,)),
            dma((2, 2)),
            dma((SWEEPS, 2)),
            dma((GROUP,)),
            dma((2, 2)),
            dma((4,)),
            dma((4,)),
        ],
        compiler_params=pltpu.CompilerParams(
            collective_id=0, has_side_effects=True, vmem_limit_bytes=48 * 1024 * 1024
        ),
    )(
        pltpu.with_memory_space_constraint(point_count, pltpu.HBM),
        box_count,
        *(
            pltpu.with_memory_space_constraint(x, pltpu.HBM)
            for x in (
                self_block,
                cross_block,
                redundant_inverse,
                link_block,
                projection,
                parent_far,
            )
        ),
    )
    return pl.pallas_call(
        settle,
        name="settle",
        out_shape=shapes,
        in_specs=[hbm] * 2,
        out_specs=(hbm, hbm),
        scratch_shapes=[dma((2,))],
    )(*(pltpu.with_memory_space_constraint(x, pltpu.VMEM) for x in results))


def solution(mesh):
    block = P(("wide", "narrow"), None, None)
    flat = P(("wide", "narrow"))
    return jax.shard_map(
        functools.partial(local, mesh.shape["wide"]),
        mesh=mesh,
        in_specs=(block,) * 6 + (flat,) * 2,
        out_specs=(block, block),
        check_vma=False,
    )
```

```python
import functools

import jax
import jax.numpy as jnp
from jax import lax
from jax.experimental import pallas as pl
from jax.experimental.pallas import tpu as pltpu
from jax.sharding import PartitionSpec as P

SWEEPS = 4
GROUP = 4
PIECES = 2
MESH = pl.DeviceIdType.MESH
F32 = jnp.float32
BF16 = jnp.bfloat16


def mm(a, b):
    return jnp.dot(a, b, preferred_element_type=F32)


def mm_t(a, b):
    return lax.dot_general(a, b, (((1,), (1,)), ((), ())), preferred_element_type=F32)


def kernel(
    n_wide,
    pc_h,
    bc_ref,
    self_h,
    cross_h,
    inv_h,
    link_h,
    proj_h,
    far_h,
    out_ref,
    par_ref,
    pc_ref,
    cross_v,
    inv_v,
    self_v,
    loc_o,
    lnk,
    lnk_m,
    lnk_t,
    st,
    fin,
    rly,
    mo,
    r_m,
    r_s,
    cnt_o,
    cnt_i,
    prj,
    ch_o,
    ch_i,
    far_v,
    edge_m,
    edge_t,
    edge_loc,
    edge_sum,
    edge_cnt,
    cnt_ld,
    ld_sem,
    far_sem,
    own_sem,
    a2a_ss,
    a2a_rs,
    cnt_ss,
    cnt_rs,
    prj_rs,
    z_ss,
    z_rs,
    ch_rs,
    last_rs,
    edge_ss,
    edge_rs,
):
    k = self_h.shape[1]
    half = k // 2
    w = lax.axis_index("wide")
    n = lax.axis_index("narrow")
    y = lax.rem(w, GROUP)
    base = w - y
    b = lax.rem(n, 2)
    n0 = n - b
    q = y // 2
    uy = lax.rem(y + 1, GROUP)
    oy = lax.rem(y + 2, GROUP)
    dy = lax.rem(y + 3, GROUP)

    def at_z(by):
        return lax.rem(base + n_wide + GROUP * by, n_wide)

    def flag(condition):
        return jnp.where(condition, 1, 0)

    up = (base + uy, n)
    dn = (base + dy, n)
    op = (base + oy, n)
    zu = (at_z(1) + y, n)
    zd = (at_z(-1) + y, n)
    to_up = (at_z(-flag(y == 0)) + uy, n)
    to_dn = (at_z(flag(y == 3)) + dy, n)
    of_up_z = at_z(-flag(y == 2))
    of_dn_z = at_z(flag(y == 1))
    of_up = (of_up_z + uy, n)
    of_dn = (of_dn_z + dy, n)

    def rcopy(src, dst, ssem, rsem, dev):
        return pltpu.make_async_remote_copy(
            src_ref=src,
            dst_ref=dst,
            send_sem=ssem,
            recv_sem=rsem,
            device_id=dev,
            device_id_type=MESH,
        )

    barrier = pltpu.get_barrier_semaphore()

    def greet(dev):
        pl.semaphore_signal(barrier, inc=1, device_id=dev, device_id_type=MESH)

    y_bit = lax.rem(y, 2)
    pair_base = at_z(2 * y_bit - 1) + y + 1 - 2 * y_bit
    for i in range(GROUP):
        for c in range(2):
            if i or c:
                greet((base + lax.rem(y + i, GROUP), n0 + lax.rem(b + c, 2)))
    greet(zu)
    greet(zd)
    greet((pair_base, n0))
    greet((pair_base, n0 + 1))

    order = (uy, dy, oy, y)
    loads = []
    for i, slot in enumerate(order):
        trio = []
        for c, (h, v) in enumerate(((cross_h, cross_v), (inv_h, inv_v), (self_h, self_v))):
            cp = pltpu.make_async_copy(h.at[slot], v.at[i], ld_sem.at[i, c])
            cp.start()
            trio.append(cp)
        loads.append(trio)
        if i == 0:
            pc_cp = pltpu.make_async_copy(pc_h, pc_ref, cnt_ld)
            pc_cp.start()

    lo, hi = pl.ds(0, half), pl.ds(half, half)

    def exchange(p, src_op, dst_op, dst_relay_up, dst_relay_dn, a, bb):
        ss, rs = a2a_ss.at[p % 2], a2a_rs.at[p]
        first, second = [], []
        for i in range(2 * PIECES):
            way, piece = i % 2, i // 2
            rows_of = pl.ds(way * half + piece * (half // PIECES), half // PIECES)
            held = rly.at[p, way, pl.ds(piece * (half // PIECES), half // PIECES)]
            dev, dst = ((up, dst_relay_up), (dn, dst_relay_dn))[way]
            first.append(rcopy(src_op.at[rows_of], held, ss.at[2 + i], rs.at[2 + i], dev))
            o = 2 + 2 * PIECES + i
            second.append(rcopy(held, dst.at[rows_of], ss.at[2 + i], rs.at[o], dev))
        return {
            2: rcopy(a[0], a[1], ss.at[0], rs.at[0], a[2]),
            3: rcopy(bb[0], bb[1], ss.at[1], rs.at[1], bb[2]),
            "first": first,
            "second": second,
        }

    def outward(p, src_up, src_dn, src_op, dst):
        return exchange(
            p,
            src_op,
            dst.at[2],
            dst.at[2],
            dst.at[2],
            (src_up, dst.at[3], to_up),
            (src_dn, dst.at[1], to_dn),
        )

    link_x = outward(0, link_h.at[uy], link_h.at[dy], link_h.at[oy], lnk)
    loc_x = outward(1, loc_o.at[0], loc_o.at[1], loc_o.at[2], st.at[0])
    fin_x = exchange(
        2,
        fin.at[2],
        out_ref.at[y],
        out_ref.at[dy],
        out_ref.at[uy],
        (fin.at[1], out_ref.at[y], of_up),
        (fin.at[3], out_ref.at[y], of_dn),
    )

    last_lo, last_hi = (
        [
            rcopy(fin.at[o, part], out_ref.at[y, part], a2a_ss.at[1, i], last_rs.at[v, i], dev)
            for v, (o, dev) in enumerate(((3, of_dn), (1, of_up)))
        ]
        for i, part in enumerate((lo, hi))
    )

    def relay(ex):
        for a, b_ in zip(ex["first"], ex["second"]):
            a.wait_recv()
            a.wait_send()
            b_.start()

    pc_cp.wait()
    live = bc_ref[0]
    effs = []
    for i, slot in enumerate(order):
        eff = jnp.where(slot < live, pc_ref[slot], 0)
        effs.append(eff)
        if i < 3:
            cnt_o[i] = jnp.full((8, 128), eff, jnp.int32)
        else:
            cnt_i[0] = jnp.full((8, 128), eff, jnp.int32)

    pl.semaphore_wait(barrier, 2 * GROUP + 3)
    cnt_x = []
    for i, (rel, dev) in enumerate(((3, to_up), (1, to_dn), (2, op))):
        cp = rcopy(cnt_o.at[i], cnt_i.at[rel], cnt_ss.at[i], cnt_rs.at[i], dev)
        cp.start()
        cnt_x.append(cp)
    link_x[2].start()
    link_x[3].start()
    own_link = pltpu.make_async_copy(link_h.at[y], lnk.at[0], own_sem.at[0])
    own_link.start()
    own_prj = pltpu.make_async_copy(proj_h.at[y], prj.at[0], own_sem.at[1])
    own_prj.start()
    far_cp = pltpu.make_async_copy(far_h.at[0], far_v, far_sem)
    far_cp.start()

    rows = lax.broadcasted_iota(jnp.int32, (k, k), 0)
    cols = lax.broadcasted_iota(jnp.int32, (k, k), 1)

    def schur(i):
        for cp in loads[i]:
            cp.wait()
        cross = cross_v[i]
        carried = mm(cross, inv_v[i]).astype(BF16)
        update = mm_t(carried, cross)
        inside = (rows < effs[i]) & (cols < effs[i])
        return jnp.where(inside, self_v[i].astype(F32) - update, 0.0).astype(BF16)

    loc_o[0] = schur(0)
    loc_o[1] = schur(1)
    loc_x[2].start()
    loc_x[3].start()
    loc_o[2] = schur(2)
    for ex in (link_x, loc_x):
        for cp in ex["first"]:
            cp.start()
    st[0, 0] = schur(3)

    def origin(j):
        return lax.rem(q + j, GROUP)

    own_link.wait()
    for cp in cnt_x:
        cp.wait_recv()

    def count(j):
        return cnt_i[pl.ds(origin(j), 1), 0:1, 0:1][0]

    def prepare(j, last):
        inside = rows < count(j)
        if not last:
            inside = inside & (cols < count(j + 1))
        masked = jnp.where(inside, lnk[pl.ds(origin(j), 1)][0].astype(F32), 0.0)
        lnk_m[pl.ds(j, 1)] = masked.astype(BF16)[None]
        lnk_t[pl.ds(j, 1)] = masked.T.astype(BF16)[None]

    def state(t, j):
        return st[t, pl.ds(origin(j) if t == 0 else j, 1)][0]

    def at(ref, j):
        return ref[pl.ds(j, 1)][0]

    def lower(t, j):
        return mm(at(lnk_t, j), mm(state(t, j), at(lnk_m, j)).astype(BF16)).astype(BF16)

    def upper(above, j):
        return mm(at(lnk_m, j), mm(above, at(lnk_t, j)).astype(BF16))

    def down_copy(t):
        src = st.at[0, origin(0)] if t == 0 else st.at[2, 1] if t == 3 else st.at[t, 0]
        return rcopy(src, r_s.at[t], z_ss.at[t % 2, 0], z_rs.at[t, 0], zd)

    def up_copy(t):
        return rcopy(mo.at[t], r_m.at[t], z_ss.at[t % 2, 1], z_rs.at[t, 1], zu)

    def when_type(i, copies):
        for v in range(2):

            @pl.when(q == v)
            def _():
                copies[i + (v if i == 2 else -v)].wait_recv()

    when_type(2, link_x)
    prepare(3, True)
    prepare(0, False)
    edge_x = [
        rcopy(src, dst, edge_ss.at[i], edge_rs.at[i], dev)
        for i, (src, dst, dev) in enumerate(
            (
                (lnk_m.at[3], edge_m.at[0], zu),
                (lnk_m.at[0], edge_m.at[1], zd),
                (cnt_i.at[origin(0)], edge_cnt, zd),
                (st.at[0, origin(3)], edge_loc, zu),
            )
        )
    ]
    edge_x[0].start()
    when_type(2, loc_x)
    down_copy(0).start()
    mo[0] = lower(0, 3)
    up_copy(0).start()
    edge_x[3].start()
    edge_x[1].start()
    edge_x[2].start()
    relay(link_x)
    when_type(3, link_x)
    prepare(1 + q, False)
    relay(loc_x)
    for cp in link_x["second"]:
        cp.wait_recv()
    prepare(2 - q, False)
    when_type(3, loc_x)
    down_copy(0).wait_recv()
    top = upper(r_s[0], 3)
    up_copy(0).wait_recv()
    def combine(t, j, low, high):
        total = state(0, j).astype(F32) - low.astype(F32) - high
        if t == SWEEPS - 1:
            total = total + jnp.where((rows == cols) & (rows >= count(j)), 1.0, 0.0)
            fin[pl.ds(origin(j), 1)] = total.astype(BF16)[None]
        else:
            st[t + 1, j] = total.astype(BF16)

    own_out = pltpu.make_async_copy(fin.at[0], out_ref.at[y], own_sem.at[2])
    kp = prj.shape[1]
    lane_half = lax.broadcasted_iota(jnp.int32, (1, 2 * kp), 1) // kp

    def child_copies(rel):
        from_y = lax.rem(y + rel, GROUP)
        from_base = jnp.where(rel == 1, of_up_z, jnp.where(rel == 3, of_dn_z, base))
        c = 2 * lax.rem(from_y, 2) + b
        owner_y = 2 * (from_y // 2) + q
        dev = (from_base + owner_y, n0 + y_bit)
        mine = (from_base == base) & (owner_y == y) & (b == y_bit)
        here = pltpu.make_async_copy(ch_o.at[rel], ch_i.at[c], ch_rs.at[c])
        there = rcopy(ch_o.at[rel], ch_i.at[c], a2a_ss.at[1, 2 + rel], ch_rs.at[c], dev)
        return mine, here, there

    def children(*rels):
        for rel in rels:
            p = at(prj, rel)
            kept = mm(p, at(fin, rel)).astype(BF16)
            both = mm_t(kept, jnp.concatenate([p, p], axis=0))
            ch_o[pl.ds(rel, 1)] = jnp.where(lane_half == b, both, 0.0).astype(BF16)[None]
        for rel in rels:
            send_child(*child_copies(rel))

    def send_child(mine, here, there):
        @pl.when(mine)
        def _():
            here.start()

        @pl.when(jnp.logical_not(mine))
        def _():
            there.start()

    def halo_low(term):
        inside = (rows < count(0)) & (cols < count(0))
        return jnp.where(inside, term.astype(F32), 0.0)

    def bottom_done(t, high):
        combine(t, 0, halo_low(r_m[t]), high)
        down_copy(t + 1).start()

    def top_done(t, low, high):
        combine(t, 3, low, high)
        mo[t + 1] = lower(t + 1, 3)
        up_copy(t + 1).start()

    @pl.when(q == 0)
    def _():
        bottom_done(0, upper(state(0, 1), 0))

    @pl.when(q == 1)
    def _():
        top_done(0, lower(0, 2), top)

    for cp in loc_x["second"]:
        cp.wait_recv()

    @pl.when(q == 0)
    def _():
        top_done(0, lower(0, 2), top)

    @pl.when(q == 1)
    def _():
        bottom_done(0, upper(state(0, 1), 0))

    for cp in cnt_x:
        cp.wait_send()
    prj_x = []
    for i, (src, rel, dev) in enumerate(((uy, 3, to_up), (dy, 1, to_dn), (oy, 2, op))):
        cp = rcopy(proj_h.at[src], prj.at[rel], cnt_ss.at[i], prj_rs.at[i], dev)
        cp.start()
        prj_x.append(cp)
    combine(0, 1, lower(0, 0), upper(state(0, 2), 1))
    combine(0, 2, lower(0, 1), upper(state(0, 3), 2))
    combine(1, 1, lower(1, 0), upper(st[1, 2], 1))
    combine(1, 2, lower(1, 1), upper(st[1, 3], 2))
    low = lower(1, 2)
    high = upper(st[1, 1], 0)
    mo[3] = lower(2, 2)
    for ex in (link_x, loc_x):
        for cp in [ex[2], ex[3]] + ex["second"]:
            cp.wait_send()
    down_copy(1).wait_recv()
    combine(1, 3, low, upper(r_s[1], 3))
    mo[2] = lower(2, 3)
    for v in range(2):
        up_copy(v).wait_send()
    up_copy(2).start()
    up_copy(3).start()
    up_copy(1).wait_recv()
    combine(1, 0, halo_low(r_m[1]), high)
    for v in range(2):
        down_copy(v).wait_send()
    down_copy(2).start()
    down_copy(3).start()
    combine(2, 1, lower(2, 0), upper(st[2, 2], 1))
    combine(2, 2, lower(2, 1), upper(st[2, 3], 2))
    for cp in edge_x:
        cp.wait_recv()
    for i in range(2):
        edge_t[i] = edge_m[i].astype(F32).T.astype(BF16)
    edge_high = mm(edge_m[0], mm(st[2, 0], edge_t[0]).astype(BF16))
    edge_sum[0] = edge_loc[...].astype(F32) - edge_high
    edge_inside = (rows < edge_cnt[0:1, 0:1]) & (cols < edge_cnt[0:1, 0:1])
    edge_sum[1] = r_s[0].astype(F32) - jnp.where(edge_inside, mo[2].astype(F32), 0.0)
    high_2 = upper(st[2, 1], 0)
    t = SWEEPS - 1
    low = lower(t, 2)
    high = upper(st[t, 1], 0)
    inner_low = lower(t, 1)
    inner_high = upper(st[t, 2], 1)

    def interior(j):
        if j == 1:
            combine(t, 1, lower(t, 0), inner_high)
        else:
            combine(t, 2, inner_low, upper(st[t, 3], 2))

    def new_top():
        down_copy(2).wait_recv()
        combine(2, 3, mo[3], upper(r_s[2], 3))

    def new_bottom():
        up_copy(2).wait_recv()
        combine(2, 0, halo_low(r_m[2]), high_2)

    def far_back():
        for cp in fin_x["first"]:
            cp.start()

    @pl.when(q == 0)
    def _():
        new_top()
        interior(2)
        far_back()
        new_bottom()
        interior(1)
        fin_x[2].start()

    @pl.when(q == 1)
    def _():
        new_bottom()
        interior(1)
        far_back()
        new_top()
        interior(2)
        fin_x[3].start()

    own_prj.wait()
    for cp in prj_x:
        cp.wait_recv()

    def last_top():
        down_copy(t).wait_recv()
        above = edge_sum[1] - mm(edge_m[1], mm(r_s[t], edge_t[1]).astype(BF16))
        combine(t, 3, low, upper(above.astype(BF16), 3))

    def last_bottom():
        up_copy(t).wait_recv()
        below = (edge_sum[0] - r_m[t].astype(F32)).astype(BF16)
        below_low = mm(edge_t[0], mm(below, edge_m[0]).astype(BF16)).astype(BF16)
        combine(t, 0, halo_low(below_low), high)

    for v, steps in enumerate(((last_top, last_bottom), (last_bottom, last_top))):

        @pl.when(q == v)
        def _():
            steps[0]()
            last_lo[v].start()
            children(1, 2, 3)
            last_hi[v].start()
            steps[1]()
            children(0)

    own_out.start()
    relay(fin_x)
    far_cp.wait()
    for c in range(4):
        pltpu.make_async_copy(ch_o.at[0], ch_i.at[c], ch_rs.at[c]).wait()
        r = pl.ds(kp * c, kp)
        l = pl.ds(2 * kp * (c // 2), 2 * kp)
        far_v[r, l] = (far_v[r, l].astype(F32) + ch_i[c].astype(F32)).astype(BF16)
    par_cp = pltpu.make_async_copy(far_v, par_ref.at[0], far_sem)
    par_cp.start()

    for cp in fin_x["second"]:
        cp.wait_recv()
    outer = (y == 0) | (y == GROUP - 1)

    @pl.when(outer)
    def _():
        for i in range(2):
            last_lo[i].wait_recv()
            last_hi[i].wait_recv()

    @pl.when(jnp.logical_not(outer))
    def _():
        fin_x[2].wait_recv()
        fin_x[3].wait_recv()

    own_out.wait()
    par_cp.wait()
    for cp in fin_x["second"]:
        cp.wait_send()
    for v in range(2):

        @pl.when(q == v)
        def _():
            fin_x[2 + v].wait_send()
            last_lo[v].wait_send()
            last_hi[v].wait_send()

    for cp in prj_x:
        cp.wait_send()
    for cp in edge_x:
        cp.wait_send()
    for t in range(2, SWEEPS):
        down_copy(t).wait_send()
        up_copy(t).wait_send()
    for rel in range(GROUP):
        mine, _, there = child_copies(rel)

        @pl.when(jnp.logical_not(mine))
        def _():
            there.wait_send()


def settle(out_v, par_v, out_h, par_h, sem):
    copies = (
        pltpu.make_async_copy(out_v, out_h, sem.at[0]),
        pltpu.make_async_copy(par_v, par_h, sem.at[1]),
    )
    for cp in copies:
        cp.start()
    for cp in copies:
        cp.wait()


def local(
    n_wide,
    self_block,
    cross_block,
    redundant_inverse,
    link_block,
    projection,
    parent_far,
    point_count,
    box_count,
):
    slots, k, r = cross_block.shape
    kp = projection.shape[1]
    hbm = pl.BlockSpec(memory_space=pl.ANY)
    smem = pl.BlockSpec(memory_space=pltpu.SMEM)
    dma = pltpu.SemaphoreType.DMA
    shapes = (
        jax.ShapeDtypeStruct(self_block.shape, BF16),
        jax.ShapeDtypeStruct(parent_far.shape, BF16),
    )
    results = pl.pallas_call(
        functools.partial(kernel, n_wide),
        name="skeleton",
        out_shape=shapes,
        in_specs=[hbm, smem] + [hbm] * 6,
        out_specs=(hbm, hbm),
        scratch_shapes=[
            pltpu.SMEM((slots,), jnp.int32),
            pltpu.VMEM((slots, k, r), BF16),
            pltpu.VMEM((slots, r, r), BF16),
            pltpu.VMEM((slots, k, k), BF16),
            pltpu.VMEM((3, k, k), BF16),
            pltpu.VMEM((GROUP, k, k), BF16),
            pltpu.VMEM((GROUP, k, k), BF16),
            pltpu.VMEM((GROUP, k, k), BF16),
            pltpu.VMEM((SWEEPS, GROUP, k, k), BF16),
            pltpu.VMEM((GROUP, k, k), BF16),
            pltpu.VMEM((3, 2, k // 2, k), BF16),
            pltpu.VMEM((SWEEPS, k, k), BF16),
            pltpu.VMEM((SWEEPS, k, k), BF16),
            pltpu.VMEM((SWEEPS, k, k), BF16),
            pltpu.VMEM((GROUP, 8, 128), jnp.int32),
            pltpu.VMEM((GROUP, 8, 128), jnp.int32),
            pltpu.VMEM((GROUP, kp, k), BF16),
            pltpu.VMEM((GROUP, kp, 2 * kp), BF16),
            pltpu.VMEM((GROUP, kp, 2 * kp), BF16),
            pltpu.VMEM((k, k), BF16),
            pltpu.VMEM((2, k, k), BF16),
            pltpu.VMEM((2, k, k), BF16),
            pltpu.VMEM((k, k), BF16),
            pltpu.VMEM((2, k, k), F32),
            pltpu.VMEM((8, 128), jnp.int32),
            dma,
            dma((4, 3)),
            dma,
            dma((3,)),
            dma((2, 2 + 2 * PIECES)),
            dma((3, 2 + 4 * PIECES)),
            dma((3,)),
            dma((3,)),
            dma((3,)),
            dma((2, 2)),
            dma((SWEEPS, 2)),
            dma((GROUP,)),
            dma((2, 2)),
            dma((4,)),
            dma((4,)),
        ],
        compiler_params=pltpu.CompilerParams(
            collective_id=0, has_side_effects=True, vmem_limit_bytes=48 * 1024 * 1024
        ),
    )(
        pltpu.with_memory_space_constraint(point_count, pltpu.HBM),
        box_count,
        *(
            pltpu.with_memory_space_constraint(x, pltpu.HBM)
            for x in (
                self_block,
                cross_block,
                redundant_inverse,
                link_block,
                projection,
                parent_far,
            )
        ),
    )
    return pl.pallas_call(
        settle,
        name="settle",
        out_shape=shapes,
        in_specs=[hbm] * 2,
        out_specs=(hbm, hbm),
        scratch_shapes=[dma((2,))],
    )(*(pltpu.with_memory_space_constraint(x, pltpu.VMEM) for x in results))


def solution(mesh):
    block = P(("wide", "narrow"), None, None)
    flat = P(("wide", "narrow"))
    return jax.shard_map(
        functools.partial(local, mesh.shape["wide"]),
        mesh=mesh,
        in_specs=(block,) * 6 + (flat,) * 2,
        out_specs=(block, block),
        check_vma=False,
    )
```

```python
import functools

import jax
import jax.numpy as jnp
from jax import lax
from jax.experimental import pallas as pl
from jax.experimental.pallas import tpu as pltpu
from jax.sharding import PartitionSpec as P

SWEEPS = 4
GROUP = 4
PIECES = 2
MESH = pl.DeviceIdType.MESH
F32 = jnp.float32
BF16 = jnp.bfloat16


def mm(a, b):
    return jnp.dot(a, b, preferred_element_type=F32)


def mm_t(a, b):
    return lax.dot_general(a, b, (((1,), (1,)), ((), ())), preferred_element_type=F32)


def kernel(
    n_wide,
    pc_h,
    bc_ref,
    self_h,
    cross_h,
    inv_h,
    link_h,
    proj_h,
    far_h,
    out_ref,
    par_ref,
    pc_ref,
    cross_v,
    inv_v,
    self_v,
    loc_o,
    lnk,
    lnk_m,
    lnk_t,
    st,
    fin,
    rly,
    mo,
    r_m,
    r_s,
    cnt_o,
    cnt_i,
    prj,
    ch_o,
    ch_i,
    far_v,
    edge_m,
    edge_t,
    edge_loc,
    edge_sum,
    edge_cnt,
    cnt_ld,
    ld_sem,
    far_sem,
    own_sem,
    a2a_ss,
    a2a_rs,
    cnt_ss,
    cnt_rs,
    prj_rs,
    z_ss,
    z_rs,
    ch_rs,
    last_rs,
    edge_ss,
    edge_rs,
):
    k = self_h.shape[1]
    half = k // 2
    w = lax.axis_index("wide")
    n = lax.axis_index("narrow")
    y = lax.rem(w, GROUP)
    base = w - y
    b = lax.rem(n, 2)
    n0 = n - b
    q = y // 2
    uy = lax.rem(y + 1, GROUP)
    oy = lax.rem(y + 2, GROUP)
    dy = lax.rem(y + 3, GROUP)

    def at_z(by):
        return lax.rem(base + n_wide + GROUP * by, n_wide)

    def flag(condition):
        return jnp.where(condition, 1, 0)

    up = (base + uy, n)
    dn = (base + dy, n)
    op = (base + oy, n)
    zu = (at_z(1) + y, n)
    zd = (at_z(-1) + y, n)
    to_up = (at_z(-flag(y == 0)) + uy, n)
    to_dn = (at_z(flag(y == 3)) + dy, n)
    of_up_z = at_z(-flag(y == 2))
    of_dn_z = at_z(flag(y == 1))
    of_up = (of_up_z + uy, n)
    of_dn = (of_dn_z + dy, n)

    def rcopy(src, dst, ssem, rsem, dev):
        return pltpu.make_async_remote_copy(
            src_ref=src,
            dst_ref=dst,
            send_sem=ssem,
            recv_sem=rsem,
            device_id=dev,
            device_id_type=MESH,
        )

    barrier = pltpu.get_barrier_semaphore()

    def greet(dev):
        pl.semaphore_signal(barrier, inc=1, device_id=dev, device_id_type=MESH)

    y_bit = lax.rem(y, 2)
    pair_base = at_z(2 * y_bit - 1) + y + 1 - 2 * y_bit
    for i in range(GROUP):
        for c in range(2):
            if i or c:
                greet((base + lax.rem(y + i, GROUP), n0 + lax.rem(b + c, 2)))
    greet(zu)
    greet(zd)
    greet((pair_base, n0))
    greet((pair_base, n0 + 1))

    order = (uy, dy, oy, y)
    loads = []
    for i, slot in enumerate(order):
        trio = []
        for c, (h, v) in enumerate(((cross_h, cross_v), (inv_h, inv_v), (self_h, self_v))):
            cp = pltpu.make_async_copy(h.at[slot], v.at[i], ld_sem.at[i, c])
            cp.start()
            trio.append(cp)
        loads.append(trio)
        if i == 0:
            pc_cp = pltpu.make_async_copy(pc_h, pc_ref, cnt_ld)
            pc_cp.start()

    lo, hi = pl.ds(0, half), pl.ds(half, half)

    def exchange(p, src_op, dst_op, dst_relay_up, dst_relay_dn, a, bb):
        ss, rs = a2a_ss.at[p % 2], a2a_rs.at[p]
        first, second = [], []
        for i in range(2 * PIECES):
            way, piece = i % 2, i // 2
            rows_of = pl.ds(way * half + piece * (half // PIECES), half // PIECES)
            held = rly.at[p, way, pl.ds(piece * (half // PIECES), half // PIECES)]
            dev, dst = ((up, dst_relay_up), (dn, dst_relay_dn))[way]
            first.append(rcopy(src_op.at[rows_of], held, ss.at[2 + i], rs.at[2 + i], dev))
            o = 2 + 2 * PIECES + i
            second.append(rcopy(held, dst.at[rows_of], ss.at[2 + i], rs.at[o], dev))
        return {
            2: rcopy(a[0], a[1], ss.at[0], rs.at[0], a[2]),
            3: rcopy(bb[0], bb[1], ss.at[1], rs.at[1], bb[2]),
            "first": first,
            "second": second,
        }

    def outward(p, src_up, src_dn, src_op, dst):
        return exchange(
            p,
            src_op,
            dst.at[2],
            dst.at[2],
            dst.at[2],
            (src_up, dst.at[3], to_up),
            (src_dn, dst.at[1], to_dn),
        )

    link_x = outward(0, link_h.at[uy], link_h.at[dy], link_h.at[oy], lnk)
    loc_x = outward(1, loc_o.at[0], loc_o.at[1], loc_o.at[2], st.at[0])
    fin_x = exchange(
        2,
        fin.at[2],
        out_ref.at[y],
        out_ref.at[dy],
        out_ref.at[uy],
        (fin.at[1], out_ref.at[y], of_up),
        (fin.at[3], out_ref.at[y], of_dn),
    )

    last_lo, last_hi = (
        [
            rcopy(fin.at[o, part], out_ref.at[y, part], a2a_ss.at[1, i], last_rs.at[v, i], dev)
            for v, (o, dev) in enumerate(((3, of_dn), (1, of_up)))
        ]
        for i, part in enumerate((lo, hi))
    )

    def relay(ex):
        for a, b_ in zip(ex["first"], ex["second"]):
            a.wait_recv()
            a.wait_send()
            b_.start()

    pc_cp.wait()
    live = bc_ref[0]
    effs = []
    for i, slot in enumerate(order):
        eff = jnp.where(slot < live, pc_ref[slot], 0)
        effs.append(eff)
        if i < 3:
            cnt_o[i] = jnp.full((8, 128), eff, jnp.int32)
        else:
            cnt_i[0] = jnp.full((8, 128), eff, jnp.int32)

    pl.semaphore_wait(barrier, 2 * GROUP + 3)
    cnt_x = []
    for i, (rel, dev) in enumerate(((3, to_up), (1, to_dn), (2, op))):
        cp = rcopy(cnt_o.at[i], cnt_i.at[rel], cnt_ss.at[i], cnt_rs.at[i], dev)
        cp.start()
        cnt_x.append(cp)
    link_x[2].start()
    link_x[3].start()
    own_link = pltpu.make_async_copy(link_h.at[y], lnk.at[0], own_sem.at[0])
    own_link.start()
    own_prj = pltpu.make_async_copy(proj_h.at[y], prj.at[0], own_sem.at[1])
    own_prj.start()
    far_cp = pltpu.make_async_copy(far_h.at[0], far_v, far_sem)
    far_cp.start()

    rows = lax.broadcasted_iota(jnp.int32, (k, k), 0)
    cols = lax.broadcasted_iota(jnp.int32, (k, k), 1)

    def schur(i):
        for cp in loads[i]:
            cp.wait()
        cross = cross_v[i]
        carried = mm(cross, inv_v[i]).astype(BF16)
        update = mm_t(carried, cross)
        inside = (rows < effs[i]) & (cols < effs[i])
        return jnp.where(inside, self_v[i].astype(F32) - update, 0.0).astype(BF16)

    loc_o[0] = schur(0)
    loc_o[1] = schur(1)
    loc_x[2].start()
    loc_x[3].start()
    loc_o[2] = schur(2)
    for ex in (link_x, loc_x):
        for cp in ex["first"]:
            cp.start()
    st[0, 0] = schur(3)

    def origin(j):
        return lax.rem(q + j, GROUP)

    own_link.wait()
    for cp in cnt_x:
        cp.wait_recv()

    def count(j):
        return cnt_i[pl.ds(origin(j), 1), 0:1, 0:1][0]

    def prepare(j, last):
        inside = rows < count(j)
        if not last:
            inside = inside & (cols < count(j + 1))
        masked = jnp.where(inside, lnk[pl.ds(origin(j), 1)][0].astype(F32), 0.0)
        lnk_m[pl.ds(j, 1)] = masked.astype(BF16)[None]
        lnk_t[pl.ds(j, 1)] = masked.T.astype(BF16)[None]

    def state(t, j):
        return st[t, pl.ds(origin(j) if t == 0 else j, 1)][0]

    def at(ref, j):
        return ref[pl.ds(j, 1)][0]

    def lower(t, j):
        return mm(at(lnk_t, j), mm(state(t, j), at(lnk_m, j)).astype(BF16)).astype(BF16)

    def upper(above, j):
        return mm(at(lnk_m, j), mm(above, at(lnk_t, j)).astype(BF16))

    def down_copy(t):
        src = st.at[0, origin(0)] if t == 0 else st.at[2, 1] if t == 3 else st.at[t, 0]
        return rcopy(src, r_s.at[t], z_ss.at[t % 2, 0], z_rs.at[t, 0], zd)

    def up_copy(t):
        return rcopy(mo.at[t], r_m.at[t], z_ss.at[t % 2, 1], z_rs.at[t, 1], zu)

    def when_type(i, copies):
        for v in range(2):

            @pl.when(q == v)
            def _():
                copies[i + (v if i == 2 else -v)].wait_recv()

    when_type(2, link_x)
    prepare(3, True)
    prepare(0, False)
    edge_x = [
        rcopy(src, dst, edge_ss.at[i], edge_rs.at[i], dev)
        for i, (src, dst, dev) in enumerate(
            (
                (lnk_m.at[3], edge_m.at[0], zu),
                (lnk_m.at[0], edge_m.at[1], zd),
                (cnt_i.at[origin(0)], edge_cnt, zd),
                (st.at[0, origin(3)], edge_loc, zu),
            )
        )
    ]
    edge_x[0].start()
    when_type(2, loc_x)
    down_copy(0).start()
    mo[0] = lower(0, 3)
    up_copy(0).start()
    edge_x[3].start()
    edge_x[1].start()
    edge_x[2].start()
    relay(link_x)
    when_type(3, link_x)
    prepare(1 + q, False)
    relay(loc_x)
    for cp in link_x["second"]:
        cp.wait_recv()
    prepare(2 - q, False)
    when_type(3, loc_x)
    down_copy(0).wait_recv()
    top = upper(r_s[0], 3)
    up_copy(0).wait_recv()
    def combine(t, j, low, high):
        total = state(0, j).astype(F32) - low.astype(F32) - high
        if t == SWEEPS - 1:
            total = total + jnp.where((rows == cols) & (rows >= count(j)), 1.0, 0.0)
            fin[pl.ds(origin(j), 1)] = total.astype(BF16)[None]
        else:
            st[t + 1, j] = total.astype(BF16)

    own_out = pltpu.make_async_copy(fin.at[0], out_ref.at[y], own_sem.at[2])
    kp = prj.shape[1]
    lane_half = lax.broadcasted_iota(jnp.int32, (1, 2 * kp), 1) // kp

    def child_copies(rel):
        from_y = lax.rem(y + rel, GROUP)
        from_base = jnp.where(rel == 1, of_up_z, jnp.where(rel == 3, of_dn_z, base))
        c = 2 * lax.rem(from_y, 2) + b
        owner_y = 2 * (from_y // 2) + q
        dev = (from_base + owner_y, n0 + y_bit)
        mine = (from_base == base) & (owner_y == y) & (b == y_bit)
        here = pltpu.make_async_copy(ch_o.at[rel], ch_i.at[c], ch_rs.at[c])
        there = rcopy(ch_o.at[rel], ch_i.at[c], a2a_ss.at[1, 2 + rel], ch_rs.at[c], dev)
        return mine, here, there

    def children(*rels):
        for rel in rels:
            p = at(prj, rel)
            kept = mm(p, at(fin, rel)).astype(BF16)
            both = mm_t(kept, jnp.concatenate([p, p], axis=0))
            ch_o[pl.ds(rel, 1)] = jnp.where(lane_half == b, both, 0.0).astype(BF16)[None]
        for rel in rels:
            send_child(*child_copies(rel))

    def send_child(mine, here, there):
        @pl.when(mine)
        def _():
            here.start()

        @pl.when(jnp.logical_not(mine))
        def _():
            there.start()

    def halo_low(term):
        inside = (rows < count(0)) & (cols < count(0))
        return jnp.where(inside, term.astype(F32), 0.0)

    def bottom_done(t, high):
        combine(t, 0, halo_low(r_m[t]), high)
        down_copy(t + 1).start()

    def top_done(t, low, high):
        combine(t, 3, low, high)
        mo[t + 1] = lower(t + 1, 3)
        up_copy(t + 1).start()

    @pl.when(q == 0)
    def _():
        bottom_done(0, upper(state(0, 1), 0))

    @pl.when(q == 1)
    def _():
        top_done(0, lower(0, 2), top)

    for cp in loc_x["second"]:
        cp.wait_recv()

    @pl.when(q == 0)
    def _():
        top_done(0, lower(0, 2), top)

    @pl.when(q == 1)
    def _():
        bottom_done(0, upper(state(0, 1), 0))

    for cp in cnt_x:
        cp.wait_send()
    prj_x = []
    for i, (src, rel, dev) in enumerate(((uy, 3, to_up), (dy, 1, to_dn), (oy, 2, op))):
        cp = rcopy(proj_h.at[src], prj.at[rel], cnt_ss.at[i], prj_rs.at[i], dev)
        cp.start()
        prj_x.append(cp)
    combine(0, 1, lower(0, 0), upper(state(0, 2), 1))
    combine(0, 2, lower(0, 1), upper(state(0, 3), 2))
    combine(1, 1, lower(1, 0), upper(st[1, 2], 1))
    combine(1, 2, lower(1, 1), upper(st[1, 3], 2))
    low = lower(1, 2)
    high = upper(st[1, 1], 0)
    mo[3] = lower(2, 2)
    for ex in (link_x, loc_x):
        for cp in [ex[2], ex[3]] + ex["second"]:
            cp.wait_send()
    down_copy(1).wait_recv()
    combine(1, 3, low, upper(r_s[1], 3))
    mo[2] = lower(2, 3)
    for v in range(2):
        up_copy(v).wait_send()
    up_copy(2).start()
    up_copy(3).start()
    up_copy(1).wait_recv()
    combine(1, 0, halo_low(r_m[1]), high)
    for v in range(2):
        down_copy(v).wait_send()
    down_copy(2).start()
    down_copy(3).start()
    combine(2, 1, lower(2, 0), upper(st[2, 2], 1))
    combine(2, 2, lower(2, 1), upper(st[2, 3], 2))
    for cp in edge_x:
        cp.wait_recv()
    for i in range(2):
        edge_t[i] = edge_m[i].astype(F32).T.astype(BF16)
    edge_high = mm(edge_m[0], mm(st[2, 0], edge_t[0]).astype(BF16))
    edge_sum[0] = edge_loc[...].astype(F32) - edge_high
    edge_inside = (rows < edge_cnt[0:1, 0:1]) & (cols < edge_cnt[0:1, 0:1])
    edge_sum[1] = r_s[0].astype(F32) - jnp.where(edge_inside, mo[2].astype(F32), 0.0)
    high_2 = upper(st[2, 1], 0)
    t = SWEEPS - 1
    low = lower(t, 2)
    high = upper(st[t, 1], 0)
    inner_low = lower(t, 1)
    inner_high = upper(st[t, 2], 1)

    def interior(j):
        if j == 1:
            combine(t, 1, lower(t, 0), inner_high)
        else:
            combine(t, 2, inner_low, upper(st[t, 3], 2))

    def new_top():
        down_copy(2).wait_recv()
        combine(2, 3, mo[3], upper(r_s[2], 3))

    def new_bottom():
        up_copy(2).wait_recv()
        combine(2, 0, halo_low(r_m[2]), high_2)

    def far_back():
        for cp in fin_x["first"]:
            cp.start()

    @pl.when(q == 0)
    def _():
        new_top()
        interior(2)
        far_back()
        new_bottom()
        interior(1)
        fin_x[2].start()

    @pl.when(q == 1)
    def _():
        new_bottom()
        interior(1)
        far_back()
        new_top()
        interior(2)
        fin_x[3].start()

    own_prj.wait()
    for cp in prj_x:
        cp.wait_recv()

    def last_top():
        down_copy(t).wait_recv()
        above = edge_sum[1] - mm(edge_m[1], mm(r_s[t], edge_t[1]).astype(BF16))
        combine(t, 3, low, upper(above.astype(BF16), 3))

    def last_bottom():
        up_copy(t).wait_recv()
        below = (edge_sum[0] - r_m[t].astype(F32)).astype(BF16)
        below_low = mm(edge_t[0], mm(below, edge_m[0]).astype(BF16)).astype(BF16)
        combine(t, 0, halo_low(below_low), high)

    for v, steps in enumerate(((last_top, last_bottom), (last_bottom, last_top))):

        @pl.when(q == v)
        def _():
            steps[0]()
            last_lo[v].start()
            children(1, 2, 3)
            last_hi[v].start()
            steps[1]()
            children(0)

    own_out.start()
    relay(fin_x)
    far_cp.wait()
    for c in range(4):
        pltpu.make_async_copy(ch_o.at[0], ch_i.at[c], ch_rs.at[c]).wait()
        r = pl.ds(kp * c, kp)
        l = pl.ds(2 * kp * (c // 2), 2 * kp)
        far_v[r, l] = (far_v[r, l].astype(F32) + ch_i[c].astype(F32)).astype(BF16)
    par_cp = pltpu.make_async_copy(far_v, par_ref.at[0], far_sem)
    par_cp.start()

    for cp in fin_x["second"]:
        cp.wait_recv()
    outer = (y == 0) | (y == GROUP - 1)

    @pl.when(outer)
    def _():
        for i in range(2):
            last_lo[i].wait_recv()
            last_hi[i].wait_recv()

    @pl.when(jnp.logical_not(outer))
    def _():
        fin_x[2].wait_recv()
        fin_x[3].wait_recv()

    own_out.wait()
    par_cp.wait()
    for cp in fin_x["second"]:
        cp.wait_send()
    for v in range(2):

        @pl.when(q == v)
        def _():
            fin_x[2 + v].wait_send()
            last_lo[v].wait_send()
            last_hi[v].wait_send()

    for cp in prj_x:
        cp.wait_send()
    for cp in edge_x:
        cp.wait_send()
    for t in range(2, SWEEPS):
        down_copy(t).wait_send()
        up_copy(t).wait_send()
    for rel in range(GROUP):
        mine, _, there = child_copies(rel)

        @pl.when(jnp.logical_not(mine))
        def _():
            there.wait_send()


def settle(out_v, par_v, out_h, par_h, sem):
    slots = out_v.shape[0]
    copies = [pltpu.make_async_copy(out_v.at[i], out_h.at[i], sem.at[i]) for i in range(slots)]
    copies.append(pltpu.make_async_copy(par_v, par_h, sem.at[slots]))
    for cp in copies:
        cp.start()
    for cp in copies:
        cp.wait()


def local(
    n_wide,
    self_block,
    cross_block,
    redundant_inverse,
    link_block,
    projection,
    parent_far,
    point_count,
    box_count,
):
    slots, k, r = cross_block.shape
    kp = projection.shape[1]
    hbm = pl.BlockSpec(memory_space=pl.ANY)
    smem = pl.BlockSpec(memory_space=pltpu.SMEM)
    dma = pltpu.SemaphoreType.DMA
    shapes = (
        jax.ShapeDtypeStruct(self_block.shape, BF16),
        jax.ShapeDtypeStruct(parent_far.shape, BF16),
    )
    results = pl.pallas_call(
        functools.partial(kernel, n_wide),
        name="skeleton",
        out_shape=shapes,
        in_specs=[hbm, smem] + [hbm] * 6,
        out_specs=(hbm, hbm),
        scratch_shapes=[
            pltpu.SMEM((slots,), jnp.int32),
            pltpu.VMEM((slots, k, r), BF16),
            pltpu.VMEM((slots, r, r), BF16),
            pltpu.VMEM((slots, k, k), BF16),
            pltpu.VMEM((3, k, k), BF16),
            pltpu.VMEM((GROUP, k, k), BF16),
            pltpu.VMEM((GROUP, k, k), BF16),
            pltpu.VMEM((GROUP, k, k), BF16),
            pltpu.VMEM((SWEEPS, GROUP, k, k), BF16),
            pltpu.VMEM((GROUP, k, k), BF16),
            pltpu.VMEM((3, 2, k // 2, k), BF16),
            pltpu.VMEM((SWEEPS, k, k), BF16),
            pltpu.VMEM((SWEEPS, k, k), BF16),
            pltpu.VMEM((SWEEPS, k, k), BF16),
            pltpu.VMEM((GROUP, 8, 128), jnp.int32),
            pltpu.VMEM((GROUP, 8, 128), jnp.int32),
            pltpu.VMEM((GROUP, kp, k), BF16),
            pltpu.VMEM((GROUP, kp, 2 * kp), BF16),
            pltpu.VMEM((GROUP, kp, 2 * kp), BF16),
            pltpu.VMEM((k, k), BF16),
            pltpu.VMEM((2, k, k), BF16),
            pltpu.VMEM((2, k, k), BF16),
            pltpu.VMEM((k, k), BF16),
            pltpu.VMEM((2, k, k), F32),
            pltpu.VMEM((8, 128), jnp.int32),
            dma,
            dma((4, 3)),
            dma,
            dma((3,)),
            dma((2, 2 + 2 * PIECES)),
            dma((3, 2 + 4 * PIECES)),
            dma((3,)),
            dma((3,)),
            dma((3,)),
            dma((2, 2)),
            dma((SWEEPS, 2)),
            dma((GROUP,)),
            dma((2, 2)),
            dma((4,)),
            dma((4,)),
        ],
        compiler_params=pltpu.CompilerParams(
            collective_id=0, has_side_effects=True, vmem_limit_bytes=48 * 1024 * 1024
        ),
    )(
        pltpu.with_memory_space_constraint(point_count, pltpu.HBM),
        box_count,
        *(
            pltpu.with_memory_space_constraint(x, pltpu.HBM)
            for x in (
                self_block,
                cross_block,
                redundant_inverse,
                link_block,
                projection,
                parent_far,
            )
        ),
    )
    return pl.pallas_call(
        settle,
        name="settle",
        out_shape=shapes,
        in_specs=[hbm] * 2,
        out_specs=(hbm, hbm),
        scratch_shapes=[dma((slots + 1,))],
    )(*(pltpu.with_memory_space_constraint(x, pltpu.VMEM) for x in results))


def solution(mesh):
    block = P(("wide", "narrow"), None, None)
    flat = P(("wide", "narrow"))
    return jax.shard_map(
        functools.partial(local, mesh.shape["wide"]),
        mesh=mesh,
        in_specs=(block,) * 6 + (flat,) * 2,
        out_specs=(block, block),
        check_vma=False,
    )
```
